32 devices in a mesh: depth: 4 (over y, core), tile: 8 (over z, x).
Axes of the slice: x: 2, y: 2, z: 4, core: 2. Of those that a mesh axis runs over, the one named last changes fastest.
Arguments:
- fields: float32 [2, 128, 128, 1024], P(None, 'depth', 'tile'), may hold values from -6 to 6
- colour_palette: float32 [3, 16], replicated, may hold values from 0.05 to 1
- opacity_palette: float32 [16], replicated, may hold values from 0.2 to 3
- tf_index: int32 [256], replicated, may hold values from 0 to 15
Outputs:
- image: float32 [4, 128, 1024], P(None, 'tile', 'depth')
The draws below stay inside these ranges and needn't reach their ends.
All inputs are finite; a program needn't handle non-finite values.
Results may differ from the reference program's by a relative error of at most 0.0003.
Values sent between devices are 32-bit elements; how exact they have to be, the bound alone decides.
No kernel may reach another device: no remote copies, remote signals or barrier semaphores. Data moves between devices by JAX's collectives and lax.ppermute only.
A program may use at most 64 MiB of HBM per device.

```python
import math
import jax
import jax.numpy as jnp
import numpy as np
from jax import lax

TX = 16
NY = 1024
BINS = 256
PALETTE = 16
NX = 128
NZ = 128


def touch_ends(array, stream_key, low, top_value):
    extent = array.shape
    place = [jax.random.randint(jax.random.fold_in(stream_key, axis), (), 0, extent[axis]) for axis in range(len(extent))]
    array = array.at[tuple(place)].set(low)
    longest = extent.index(max(extent))
    place[longest] = (place[longest] + 1) % extent[longest]
    return array.at[tuple(place)].set(top_value)


def levels(stream_key, shape, shards, smallest, top_value):
    factor_of, own = 1.0, jax.random.fold_in(stream_key, 6)
    for dim, parts in shards:
        steps = jnp.exp(jax.random.uniform(jax.random.fold_in(own, dim), (parts,), jnp.float32, smallest / len(shards), top_value / len(shards)))
        factor_of = factor_of * jnp.repeat(steps, shape[dim] // parts).reshape([-1 if axis == dim else 1 for axis in range(len(shape))])
    return factor_of


def gaussian(own_key, dims, scale, limit, pieces=(), held_as=jnp.bfloat16):
    values = jax.random.normal(own_key, dims, jnp.float32) * scale
    if len(pieces) > 0:
        values = levels(own_key, dims, pieces, -0.22, 0.18) * values
    return jnp.clip(values, min=-limit, max=limit).astype(held_as)


def setup_inputs(seed: int = 0) -> dict:
    arg_keys = jax.random.split(jax.random.key(seed), 5)
    return {
        "fields": gaussian(arg_keys[0], (2, NZ, NX, NY), 1.0, 6.0, ((1, 4), (2, 8)), jnp.float32),
        "colour_palette": jnp.clip(jax.random.uniform(arg_keys[1], (3, PALETTE), jnp.float32, 0.05, 1.0), 0.05, 1.0),
        "opacity_palette": jnp.clip(jnp.exp(jax.random.uniform(arg_keys[2], (PALETTE,), jnp.float32, math.log(0.2), math.log(3.0))), 0.2, 3.0),
        "tf_index": touch_ends(jax.random.randint(arg_keys[3], (BINS,), 0, PALETTE), jax.random.fold_in(arg_keys[3], 1), 0, PALETTE - 1).astype(jnp.int32),
    }


taps_offset = np.arange(-4.0, 5.0)
gauss_bell = np.exp(-taps_offset ** 2 / 8.0)
smooth_taps = tuple((float(weight) for weight in gauss_bell / np.sqrt(np.sum(gauss_bell ** 2))))
slope_raw = taps_offset * gauss_bell
slope_taps = tuple((float(weight) for weight in slope_raw / np.sqrt(np.sum(slope_raw ** 2))))

def filter_axis(field, taps, axis):
    count = field.shape[axis] - (len(taps) - 1)
    total = taps[0] * lax.slice_in_dim(field, 0, count, axis=axis)
    for offset in range(1, len(taps)):
        total = total + taps[offset] * lax.slice_in_dim(field, offset, offset + count, axis=axis)
    return total

def smooth_three(field, first):
    for axis in range(first, first + 3):
        field = filter_axis(field, smooth_taps, axis)
    return field

def slopes(smooth_a):
    core = smooth_a[4:-4, 4:-4, 4:-4]
    grad_z = filter_axis(smooth_a[:, 4:-4, 4:-4], slope_taps, 0)
    grad_x = filter_axis(smooth_a[4:-4, :, 4:-4], slope_taps, 1)
    grad_y = filter_axis(smooth_a[4:-4, 4:-4, :], slope_taps, 2)
    return (core, grad_z, grad_x, grad_y)

def shade_march(smooth_a, smooth_b, grad_z, grad_x, grad_y, table, depth_total):
    bins = table.shape[1]
    level = (bins - 1) * jax.nn.sigmoid(1.5 * smooth_a)
    bin_index = jnp.clip(jnp.floor(level).astype(jnp.int32), 0, bins - 2)
    fraction = level - bin_index.astype(level.dtype)
    lower = jnp.take(table, bin_index, axis=1)
    upper = jnp.take(table, bin_index + 1, axis=1)
    looked = lower * (1.0 - fraction) + upper * fraction
    facing = jnp.abs(0.26726 * grad_z + 0.53452 * grad_x + 0.80178 * grad_y)
    length = jnp.sqrt(jnp.maximum(grad_z * grad_z + grad_x * grad_x + grad_y * grad_y, 0.1))
    shade = 0.3 + 0.7 * facing / length
    optical = 1.5 * (2.0 / depth_total) * looked[3] * jax.nn.sigmoid(2.0 * smooth_b)
    running = jnp.cumsum(optical, axis=0)
    total = running[-1]
    before = running - optical
    weight = jnp.exp(-before) * -jnp.expm1(-optical)
    colour = lax.optimization_barrier(jnp.sum(weight[None] * looked[:3] * shade[None], axis=1))
    return jnp.concatenate([colour, jnp.exp(-total)[None]], axis=0)

def reference(fields, colour_palette, opacity_palette, tf_index):
    table = jnp.concatenate([jnp.take(colour_palette, tf_index, axis=1), jnp.take(opacity_palette, tf_index)[None]], axis=0)
    padded = jnp.pad(fields, ((0, 0), (8, 8), (8, 8), (8, 8)))
    depth_pos = jnp.arange(NZ + 8, dtype=jnp.int32) - 4
    depth_ok = (depth_pos >= 0) & (depth_pos < NZ)
    column_pos = jnp.arange(NY + 8, dtype=jnp.int32) - 4
    column_ok = (column_pos >= 0) & (column_pos < NY)

    def one_strip(strip):
        piece = lax.dynamic_slice_in_dim(padded, (strip * TX).astype(jnp.int32), TX + 16, axis=2)
        smooth_a = smooth_three(piece[0], 0)
        row_pos = strip * TX - 4 + jnp.arange(TX + 8, dtype=jnp.int32)
        row_ok = (row_pos >= 0) & (row_pos < NX)
        inside = depth_ok[:, None, None] & row_ok[None, :, None] & column_ok[None, None, :]
        smooth_a = jnp.where(inside, smooth_a, jnp.float32(0.0))
        smooth_b = smooth_three(piece[1, 4:-4, 4:-4, 4:-4], 0)
        core, grad_z, grad_x, grad_y = slopes(smooth_a)
        return shade_march(core, smooth_b, grad_z, grad_x, grad_y, table, NZ)
    strips = lax.map(one_strip, jnp.arange(NX // TX, dtype=jnp.int32))
    return jnp.transpose(strips, (1, 0, 2, 3)).reshape(4, NX, NY)
```

```python
import functools

import jax
import jax.numpy as jnp
import ml_dtypes
import numpy as np
from jax import lax
from jax.experimental import pallas as pl
from jax.experimental.pallas import tpu as pltpu
from jax.sharding import Mesh
from jax.sharding import PartitionSpec as P

RAD = 4
LANES = 128
HALO = 8
PER = LANES // (2 * RAD)

offsets = np.arange(-4.0, 5.0)
bell = np.exp(-(offsets**2) / 8.0)
S_TAPS = bell / np.sqrt(np.sum(bell**2))
slope_raw = offsets * bell
D_TAPS = slope_raw / np.sqrt(np.sum(slope_raw**2))


def split_np(matrix):
    hi = matrix.astype(ml_dtypes.bfloat16)
    lo = (matrix - hi.astype(np.float64)).astype(ml_dtypes.bfloat16)
    return hi, lo


def split(value):
    hi = value.astype(jnp.bfloat16)
    return hi, (value - hi.astype(jnp.float32)).astype(jnp.bfloat16)


def mxu(a, b):
    return jnp.dot(a, b, preferred_element_type=jnp.float32)


def band(taps, rows, cols, shift):
    matrix = np.zeros((rows, cols))
    for row in range(rows):
        for k in range(-RAD, RAD + 1):
            if 0 <= row + k + shift < cols:
                matrix[row, row + k + shift] = taps[k + RAD]
    return matrix


def symmetric(block, n):
    t = [float(x) for x in S_TAPS[RAD:]]
    out = t[0] * block[4 : 4 + n]
    for k in range(1, RAD + 1):
        out = out + t[k] * (block[4 - k : 4 - k + n] + block[4 + k : 4 + k + n])
    return out


def slope(block, n):
    t = [float(x) for x in D_TAPS[RAD:]]
    out = t[1] * (block[5 : 5 + n] - block[3 : 3 + n])
    for k in range(2, RAD + 1):
        out = out + t[k] * (block[4 + k : 4 + k + n] - block[4 - k : 4 - k + n])
    return out


def source_kernel(blocks, edges, f_ref, bh_ref, bl_ref, o_ref):
    planes, rows, columns = f_ref.shape[1:]
    step = pl.program_id(0)
    wide = 2 * LANES
    hi, lo = split(f_ref[0].reshape(planes * rows, columns))
    for j in range(columns // wide):
        left, right = max(0, wide * j - LANES), min(columns, wide * (j + 1) + LANES)
        base = left - (wide * j - LANES)
        bh = bh_ref[base : base + right - left]
        bl = bl_ref[base : base + right - left]
        u = mxu(hi[:, left:right], bh) + mxu(lo[:, left:right], bh) + mxu(hi[:, left:right], bl)
        for h in range(2):
            o_ref[2 * j + h, pl.ds(step * planes, planes)] = u[
                :, h * LANES : (h + 1) * LANES
            ].reshape(planes, rows, LANES)
    if edges:
        total = o_ref.shape[1] - edges
        lane = lax.broadcasted_iota(jnp.int32, (rows, LANES), 1)
        zero = jnp.zeros((rows, LANES), jnp.float32)
        for b in range(blocks):
            acc = zero
            for z in range(planes):
                before = o_ref[b - 1, step * planes + z] if b > 0 else zero
                after = o_ref[b + 1, step * planes + z] if b < blocks - 1 else zero
                both = jnp.where(lane >= LANES // 2, before, after)
                moved = pltpu.roll(both, RAD + 2 * RAD * z, 1)
                acc = jnp.where(lane // (2 * RAD) == z, moved, acc)
            o_ref[b, total + step] = acc


def source(fields, which, bh, bl, edges):
    _, slab, rows, columns = fields.shape
    blocks = columns // LANES
    extra = slab // PER if edges else 0
    return pl.pallas_call(
        functools.partial(source_kernel, blocks, extra),
        grid=(slab // PER,),
        in_specs=[
            pl.BlockSpec((1, PER, rows, columns), lambda i: (which, i, 0, 0)),
            pl.BlockSpec((4 * LANES, 2 * LANES), lambda i: (0, 0)),
            pl.BlockSpec((4 * LANES, 2 * LANES), lambda i: (0, 0)),
        ],
        out_specs=pl.BlockSpec((blocks, slab + extra, rows, LANES), lambda i: (0, 0, 0, 0)),
        out_shape=jax.ShapeDtypeStruct((blocks, slab + extra, rows, LANES), jnp.float32),
        compiler_params=pltpu.CompilerParams(vmem_limit_bytes=48 << 20),
        name="columns_filter",
    )(fields, bh, bl)


def gather_rows(groups, slab, extra, r_ref, hl_ref, hr_ref, zin, ein, sems):
    depth = r_ref.shape[0] // groups
    rows = r_ref.shape[2]
    ends = zin.shape[1] - HALO
    copies = []
    parts = [(r_ref, d * groups + g, d, HALO + g * rows, rows) for d in range(depth) for g in range(groups)]
    parts += [(hl_ref, d, d, 0, HALO) for d in range(depth)]
    parts += [(hr_ref, d, d, ends, HALO) for d in range(depth)]
    for ref, block, d, row, count in parts:
        copies.append(
            pltpu.make_async_copy(
                ref.at[block, pl.ds(0, slab)],
                zin.at[pl.ds(RAD + d * slab, slab), pl.ds(row, count)],
                sems.at[len(copies)],
            )
        )
        if extra:
            copies.append(
                pltpu.make_async_copy(
                    ref.at[block, pl.ds(slab, extra)],
                    ein.at[pl.ds(1 + d * extra, extra), pl.ds(row, count)],
                    sems.at[len(copies)],
                )
            )
    for copy in copies:
        copy.start()
    return copies


def plane_smooth(zin, start, count):
    tiles = []
    for row in range(0, zin.shape[1], 8):
        tiles.append(symmetric(zin[pl.ds(start, count + 2 * RAD), row : row + 8, :], count))
    hi, lo = split(jnp.concatenate(tiles, axis=1))
    return jnp.concatenate([hi, lo, hi], axis=1)


def first_kernel(
    groups, slab, extra, r_ref, hl_ref, hr_ref, lhs_ref, yw_ref, zh_ref, zl_ref, pair_ref, pal_ref,
    o_ref, zin, ein, sm, gx, gy, es, sems,
):
    copies = gather_rows(groups, slab, extra, r_ref, hl_ref, hr_ref, zin, ein, sems)
    planes = zin.shape[0] - 2 * RAD
    rows = sm.shape[1]
    wide = zin.shape[1]
    for ref in (zin, sm):
        ref[:RAD] = jnp.zeros((RAD,) + ref.shape[1:], jnp.float32)
        ref[planes + RAD :] = jnp.zeros((RAD,) + ref.shape[1:], jnp.float32)
    ein[0] = jnp.zeros((wide, LANES), jnp.float32)
    ein[ein.shape[0] - 1] = jnp.zeros((wide, LANES), jnp.float32)
    for copy in copies:
        copy.wait()
    step = 8

    for j in range(es.shape[0]):
        hi, lo = split(jnp.concatenate([ein[j], ein[j + 1], ein[j + 2]], axis=1))
        ez = mxu(hi, zh_ref[...]) + mxu(lo, zh_ref[...]) + mxu(hi, zl_ref[...])
        hi, lo = split(ez)
        es[j] = mxu(lhs_ref[:rows], jnp.concatenate([hi, lo, hi], axis=0))

    def smooth_step(t, carry):
        start = pl.multiple_of(t * step, step)
        stack = plane_smooth(zin, start, step)
        for q in range(0, step, 2):
            out = mxu(lhs_ref[...], jnp.concatenate([stack[q], stack[q + 1]], axis=1))
            for h in range(2):
                part = out[:, h * LANES : (h + 1) * LANES]
                sm[RAD + start + q + h] = part[:rows]
                gx[start + q + h] = part[rows:]
        return carry

    lax.fori_loop(0, planes // step, smooth_step, 0)

    halves = pair_ref.shape[0]
    bins = halves * LANES
    factor = 1.5 * (2.0 / planes)

    def shade_step(t, carry):
        start = pl.multiple_of(t * step, step)
        group = es[start // PER]
        moved = []
        for i in range(step):
            shift = (LANES - 2 * RAD * (lax.rem(start, PER) + i)) % LANES
            moved.append(pltpu.roll(group, shift, 1))
        moved = jnp.concatenate(moved, axis=0)
        own = sm[pl.ds(RAD + start, step)].reshape(step * rows, LANES)
        hi, lo = split(jnp.concatenate([own, moved], axis=1))
        out = mxu(hi, yw_ref[...])
        out = out[:, :LANES] + out[:, LANES:] + mxu(lo, yw_ref[:, :LANES])
        gy[...] = out.reshape(step, rows, LANES)
        for row in range(0, rows, 8):
            block = sm[pl.ds(start, step + 2 * RAD), row : row + 8, :]
            grad_z = slope(block, step)
            grad_x = gx[pl.ds(start, step), row : row + 8, :]
            grad_y = gy[:, row : row + 8, :]
            facing = jnp.abs(0.26726 * grad_z + 0.53452 * grad_x + 0.80178 * grad_y)
            square = jnp.maximum(grad_z * grad_z + grad_x * grad_x + grad_y * grad_y, 0.1)
            shade = 0.3 + 0.7 * facing * lax.rsqrt(square)
            half = 0.5 * (bins - 1)
            level = half * jnp.tanh(0.75 * block[RAD : RAD + step]) + half
            index = jnp.minimum(level.astype(jnp.int32), bins - 2)
            fraction = level - index.astype(jnp.float32)
            for i in range(step):
                at = index[i] & (LANES - 1)
                pair = jnp.take_along_axis(
                    jnp.broadcast_to(pair_ref[0], (8, LANES)), at, axis=1, mode="promise_in_bounds"
                )
                for h in range(1, halves):
                    other = jnp.take_along_axis(
                        jnp.broadcast_to(pair_ref[h], (8, LANES)), at, axis=1, mode="promise_in_bounds"
                    )
                    pair = jnp.where(index[i] >= h * LANES, other, pair)
                low, high = pair & (LANES - 1), pair >> 7
                for c in range(4):
                    colours = jnp.broadcast_to(pal_ref[c], (8, LANES))
                    first = jnp.take_along_axis(colours, low, axis=1, mode="promise_in_bounds")
                    second = jnp.take_along_axis(colours, high, axis=1, mode="promise_in_bounds")
                    looked = first + fraction[i] * (second - first)
                    o_ref[c, start + i, row : row + 8, :] = looked * (shade[i] if c < 3 else factor)
        return carry

    lax.fori_loop(0, planes // step, shade_step, 0)


def second_kernel(groups, slab, r_ref, hl_ref, hr_ref, lhs_ref, c_ref, o_ref, zin, sm, sems):
    copies = gather_rows(groups, slab, 0, r_ref, hl_ref, hr_ref, zin, None, sems)
    planes = zin.shape[0] - 2 * RAD
    rows = o_ref.shape[1]
    zin[:RAD] = jnp.zeros((RAD,) + zin.shape[1:], jnp.float32)
    zin[planes + RAD :] = jnp.zeros((RAD,) + zin.shape[1:], jnp.float32)
    for copy in copies:
        copy.wait()
    step = 8

    def march(t, carry):
        start = pl.multiple_of(t * step, step)
        stack = plane_smooth(zin, start, step)
        for q in range(0, step, 2):
            out = mxu(lhs_ref[...], jnp.concatenate([stack[q], stack[q + 1]], axis=1))
            sm[q] = out[:, :LANES]
            sm[q + 1] = out[:, LANES:]
        through, red, green, blue = carry
        for i in range(step):
            sigmoid = 0.5 * jnp.tanh(sm[i]) + 0.5
            passed = through * jnp.exp(-(c_ref[3, start + i] * sigmoid))
            weight = through - passed
            red = red + weight * c_ref[0, start + i]
            green = green + weight * c_ref[1, start + i]
            blue = blue + weight * c_ref[2, start + i]
            through = passed
        return through, red, green, blue

    zero = jnp.zeros((rows, LANES), jnp.float32)
    through, red, green, blue = lax.fori_loop(
        0, planes // step, march, (zero + 1.0, zero, zero, zero)
    )
    for c, value in enumerate((red, green, blue, through)):
        o_ref[c] = value


def vmem_call(kernel, out_shape, scratch, in_specs, name):
    return pl.pallas_call(
        kernel,
        in_specs=in_specs,
        out_specs=pl.BlockSpec(memory_space=pltpu.VMEM),
        out_shape=jax.ShapeDtypeStruct(out_shape, jnp.float32),
        scratch_shapes=scratch,
        compiler_params=pltpu.CompilerParams(vmem_limit_bytes=56 << 20),
        name=name,
    )


def row_halo(blocks, groups, count):
    depth = blocks.shape[0] // groups
    shaped = blocks.reshape((depth, groups) + blocks.shape[1:])
    head = shaped[:, 0, :, :HALO]
    tail = shaped[:, groups - 1, :, shaped.shape[3] - HALO :]
    left = lax.ppermute(tail, "strips", [(i, i + 1) for i in range(count - 1)])
    right = lax.ppermute(head, "strips", [(i + 1, i) for i in range(count - 1)])
    return left, right


def local(depth, count, groups, fields, colour_palette, opacity_palette, tf_index):
    slab, strip, columns = fields.shape[1:]
    extra = slab // PER
    planes = slab * depth
    rows = strip * groups
    wide = rows + 2 * HALO
    bins = tf_index.shape[0]

    bh, bl = split_np(band(S_TAPS, 2 * LANES, 4 * LANES, LANES).T)
    smooth_rows = band(S_TAPS, rows + 2 * RAD, wide, HALO - RAD)
    slope_rows = band(D_TAPS, rows, rows + 2 * RAD, RAD)
    forms = []
    for case in range(4):
        inside = np.ones((rows + 2 * RAD, 1))
        if case & 1:
            inside[:RAD] = 0
        if case & 2:
            inside[-RAD:] = 0
        both = np.concatenate([smooth_rows[RAD:-RAD], slope_rows @ (inside * smooth_rows)], axis=0)
        hi, lo = split_np(both)
        forms.append(np.concatenate([hi, hi, lo], axis=1))
    place = lax.axis_index("strips")
    case = (place == 0).astype(jnp.int32) + 2 * (place == count - 1).astype(jnp.int32)
    lhs = lax.dynamic_index_in_dim(jnp.asarray(np.stack(forms)), case, 0, keepdims=False)
    across = np.zeros((2 * LANES, LANES))
    across[:LANES] = band(D_TAPS, LANES, LANES, 0).T
    for lane in range(LANES):
        for k in range(-RAD, RAD + 1):
            if lane + k < 0:
                across[LANES + lane + k + RAD, lane] = D_TAPS[k + RAD]
            if lane + k >= LANES:
                across[LANES + RAD + lane + k - LANES, lane] = D_TAPS[k + RAD]
    yw = np.concatenate(split_np(across), axis=1)
    zh, zl = split_np(np.kron(band(S_TAPS, PER, 3 * PER, PER).T, np.eye(2 * RAD)))

    following = jnp.concatenate([tf_index[1:], tf_index[-1:]])
    pair = (tf_index + LANES * following).reshape(bins // LANES, 1, LANES)
    palette = jnp.concatenate([colour_palette, opacity_palette[None]], axis=0)
    palette = jnp.pad(palette, ((0, 0), (0, LANES - palette.shape[1])))[:, None, :]

    group_axes = ("depth", "pair")
    sent0 = source(fields, 0, bh, bl, True)
    sent1 = source(fields, 1, bh, bl, False)
    got0 = lax.all_to_all(sent0, group_axes, 0, 0, tiled=True)
    left0, right0 = row_halo(got0, groups, count)
    got1 = lax.all_to_all(sent1, group_axes, 0, 0, tiled=True)
    left1, right1 = row_halo(got1, groups, count)

    anywhere = pl.BlockSpec(memory_space=pl.ANY)
    vmem = pl.BlockSpec(memory_space=pltpu.VMEM)
    f32 = jnp.float32
    parts = depth * (groups + 2)
    coloured = vmem_call(
        functools.partial(first_kernel, groups, slab, extra),
        (4, planes, rows, LANES),
        [
            pltpu.VMEM((planes + 2 * RAD, wide, LANES), f32),
            pltpu.VMEM((planes // PER + 2, wide, LANES), f32),
            pltpu.VMEM((planes + 2 * RAD, rows, LANES), f32),
            pltpu.VMEM((planes, rows, LANES), f32),
            pltpu.VMEM((8, rows, LANES), f32),
            pltpu.VMEM((planes // PER, rows, LANES), f32),
            pltpu.SemaphoreType.DMA((2 * parts,)),
        ],
        [anywhere] * 3 + [vmem] * 6,
        "gradients_and_colours",
    )(got0, left0, right0, lhs, yw, zh, zl, pair, palette)
    image = vmem_call(
        functools.partial(second_kernel, groups, slab),
        (4, rows, LANES),
        [
            pltpu.VMEM((planes + 2 * RAD, wide, LANES), f32),
            pltpu.VMEM((8, rows, LANES), f32),
            pltpu.SemaphoreType.DMA((parts,)),
        ],
        [anywhere] * 3 + [vmem] * 2,
        "march",
    )(got1, left1, right1, lhs[:rows], coloured)
    if groups == 1:
        return image
    return lax.all_to_all(image, "pair", 1, 2, tiled=True)


def solution(mesh):
    depth, tiles = mesh.devices.shape

    def program(fields, colour_palette, opacity_palette, tf_index):
        groups = max(1, fields.shape[3] // (LANES * depth))
        count = tiles // groups
        finer = Mesh(mesh.devices.reshape(depth, count, groups), ("depth", "strips", "pair"))
        return jax.shard_map(
            functools.partial(local, depth, count, groups),
            mesh=finer,
            in_specs=(P(None, "depth", ("strips", "pair"), None), P(), P(), P()),
            out_specs=P(None, ("strips", "pair"), "depth"),
            check_vma=False,
        )(fields, colour_palette, opacity_palette, tf_index)

    return program
```

```python
import functools

import jax
import jax.numpy as jnp
import ml_dtypes
import numpy as np
from jax import lax
from jax.experimental import pallas as pl
from jax.experimental.pallas import tpu as pltpu
from jax.sharding import Mesh
from jax.sharding import PartitionSpec as P

RAD = 4
LANES = 128
HALO = 8
GROUP = ("depth", "pair")
PER = LANES // (2 * RAD)

offsets = np.arange(-4.0, 5.0)
bell = np.exp(-(offsets**2) / 8.0)
S_TAPS = bell / np.sqrt(np.sum(bell**2))
slope_raw = offsets * bell
D_TAPS = slope_raw / np.sqrt(np.sum(slope_raw**2))


def split_np(matrix):
    hi = matrix.astype(ml_dtypes.bfloat16)
    lo = (matrix - hi.astype(np.float64)).astype(ml_dtypes.bfloat16)
    return hi, lo


def split(value):
    hi = value.astype(jnp.bfloat16)
    return hi, (value - hi.astype(jnp.float32)).astype(jnp.bfloat16)


def mxu(a, b):
    return jnp.dot(a, b, preferred_element_type=jnp.float32)


def band(taps, rows, cols, shift):
    matrix = np.zeros((rows, cols))
    for row in range(rows):
        for k in range(-RAD, RAD + 1):
            if 0 <= row + k + shift < cols:
                matrix[row, row + k + shift] = taps[k + RAD]
    return matrix


def symmetric(block, n):
    t = [float(x) for x in S_TAPS[RAD:]]
    out = t[0] * block[4 : 4 + n]
    for k in range(1, RAD + 1):
        out = out + t[k] * (block[4 - k : 4 - k + n] + block[4 + k : 4 + k + n])
    return out


def slope(block, n):
    t = [float(x) for x in D_TAPS[RAD:]]
    out = t[1] * (block[5 : 5 + n] - block[3 : 3 + n])
    for k in range(2, RAD + 1):
        out = out + t[k] * (block[4 + k : 4 + k + n] - block[4 - k : 4 - k + n])
    return out


def source_kernel(blocks, edges, *refs):
    f_ref, bh_ref, bl_ref = refs[:3]
    outs, (us, sems) = refs[3 : 3 + blocks], refs[3 + blocks :]
    planes, rows, columns = f_ref.shape[1:]
    step = pl.program_id(0)
    wide = 2 * LANES
    hi, lo = split(f_ref[0].reshape(planes * rows, columns))
    for j in range(columns // wide):
        left, right = max(0, wide * j - LANES), min(columns, wide * (j + 1) + LANES)
        base = left - (wide * j - LANES)
        bh = bh_ref[base : base + right - left]
        bl = bl_ref[base : base + right - left]
        u = mxu(hi[:, left:right], bh) + mxu(lo[:, left:right], bh) + mxu(hi[:, left:right], bl)
        for h in range(2):
            us[2 * j + h, pl.ds(step * planes, planes)] = u[
                :, h * LANES : (h + 1) * LANES
            ].reshape(planes, rows, LANES)
    total = us.shape[1] - edges
    if edges:
        lane = lax.broadcasted_iota(jnp.int32, (rows, LANES), 1)
        zero = jnp.zeros((rows, LANES), jnp.float32)
        for b in range(blocks):
            acc = zero
            for z in range(planes):
                before = us[b - 1, step * planes + z] if b > 0 else zero
                after = us[b + 1, step * planes + z] if b < blocks - 1 else zero
                both = jnp.where(lane >= LANES // 2, before, after)
                moved = pltpu.roll(both, RAD + 2 * RAD * z, 1)
                acc = jnp.where(lane // (2 * RAD) == z, moved, acc)
            us[b, total + step] = acc

    @pl.when(step == pl.num_programs(0) - 1)
    def _():
        me = lax.axis_index(GROUP)
        copies = [
            pltpu.make_async_copy(us.at[me ^ m], outs[m], sems.at[m]) for m in range(blocks)
        ]
        for copy in copies:
            copy.start()
        for copy in copies:
            copy.wait()


def source(fields, which, bh, bl, edges):
    _, slab, rows, columns = fields.shape
    blocks = columns // LANES
    extra = slab // PER if edges else 0
    block = (slab + extra, rows, LANES)
    return pl.pallas_call(
        functools.partial(source_kernel, blocks, extra),
        grid=(slab // PER,),
        in_specs=[
            pl.BlockSpec((1, PER, rows, columns), lambda i: (which, i, 0, 0)),
            pl.BlockSpec((4 * LANES, 2 * LANES), lambda i: (0, 0)),
            pl.BlockSpec((4 * LANES, 2 * LANES), lambda i: (0, 0)),
        ],
        out_specs=[pl.BlockSpec(memory_space=pl.ANY)] * blocks,
        out_shape=[jax.ShapeDtypeStruct(block, jnp.float32)] * blocks,
        scratch_shapes=[pltpu.VMEM((blocks,) + block, jnp.float32), pltpu.SemaphoreType.DMA((blocks,))],
        compiler_params=pltpu.CompilerParams(vmem_limit_bytes=48 << 20),
        cost_estimate=cost(5),
        name="columns_filter",
    )(fields, bh, bl)


def cost(microseconds):
    return pl.CostEstimate(flops=0, bytes_accessed=int(microseconds * 3e6), transcendentals=0)


def gather_rows(groups, slab, extra, own, halos, zin, ein, sems):
    me = lax.axis_index(GROUP)
    rows = own[0].shape[1]
    first = HALO if halos else 0
    parts = []
    for m, ref in enumerate(own):
        source_index = me ^ m
        parts.append((ref, source_index // groups, first + lax.rem(source_index, groups) * rows, rows))
    if halos:
        for i in range(halos[0].shape[0]):
            d = (me // groups) ^ i
            parts.append((halos[0].at[i], d, 0, HALO))
            parts.append((halos[1].at[i], d, zin.shape[1] - HALO, HALO))
    copies = []
    for ref, d, row, count in parts:
        row = pl.multiple_of(row, 8)
        copies.append(
            pltpu.make_async_copy(
                ref.at[pl.ds(0, slab)],
                zin.at[pl.ds(RAD + d * slab, slab), pl.ds(row, count)],
                sems.at[len(copies)],
            )
        )
        if extra:
            copies.append(
                pltpu.make_async_copy(
                    ref.at[pl.ds(slab, extra)],
                    ein.at[pl.ds(1 + d * extra, extra), pl.ds(row, count)],
                    sems.at[len(copies)],
                )
            )
    for copy in copies:
        copy.start()
    return copies


def clear_ends(ref, width):
    zero = jnp.zeros((width,) + ref.shape[1:], jnp.float32)
    ref[:width] = zero
    ref[ref.shape[0] - width :] = zero


def plane_smooth(zin, start, count):
    tiles = []
    for row in range(0, zin.shape[1], 8):
        tiles.append(symmetric(zin[pl.ds(start, count + 2 * RAD), row : row + 8, :], count))
    hi, lo = split(jnp.concatenate(tiles, axis=1))
    return jnp.concatenate([hi, lo, hi], axis=1)


def lookup(tables, index):
    return [jnp.take_along_axis(t, index, axis=1, mode="promise_in_bounds") for t in tables]


def first_kernel(groups, slab, extra, blocks, haloed, factor, *refs):
    own, refs = refs[:blocks], refs[blocks:]
    halos, refs = (refs[:2], refs[2:]) if haloed else ((), refs)
    lhs_ref, yw_ref, zh_ref, zl_ref, pair_ref, pal_ref, o_ref = refs[:7]
    zin, ein, sm, gx, gy, es, sems = refs[7:]
    copies = gather_rows(groups, slab, extra, own, halos, zin, ein, sems)
    planes = zin.shape[0] - 2 * RAD
    rows = sm.shape[1]
    wide = zin.shape[1]
    clear_ends(zin, RAD)
    clear_ends(sm, RAD)
    clear_ends(ein, 1)
    for copy in copies:
        copy.wait()
    step = 8

    near = [ein[j] for j in range(ein.shape[0])]
    count = len(near) - 2
    stacked = jnp.concatenate(
        [jnp.concatenate(near[k : k + count], axis=0) for k in range(3)], axis=1
    )
    hi, lo = split(stacked)
    ez = mxu(hi, zh_ref[...]) + mxu(lo, zh_ref[...]) + mxu(hi, zl_ref[...])
    hi, lo = split(ez.reshape(count, wide, LANES))
    stack = jnp.concatenate([hi, lo, hi], axis=1)
    for j in range(0, count, 2):
        out = mxu(lhs_ref[:rows], jnp.concatenate([stack[j], stack[j + 1]], axis=1))
        es[j] = out[:, :LANES]
        es[j + 1] = out[:, LANES:]

    def smooth_step(t, carry):
        start = pl.multiple_of(t * step, step)
        stack = plane_smooth(zin, start, step)
        for q in range(0, step, 2):
            out = mxu(lhs_ref[...], jnp.concatenate([stack[q], stack[q + 1]], axis=1))
            for h in range(2):
                part = out[:, h * LANES : (h + 1) * LANES]
                sm[RAD + start + q + h] = part[:rows]
                gx[start + q + h] = part[rows:]
        return carry

    lax.fori_loop(0, planes // step, smooth_step, 0)

    halves = pair_ref.shape[0]
    bins = halves * LANES

    def shade_step(t, carry):
        start = pl.multiple_of(t * step, step)
        group = es[start // PER]
        moved = []
        for i in range(step):
            shift = (LANES - 2 * RAD * (lax.rem(start, PER) + i)) % LANES
            moved.append(pltpu.roll(group, shift, 1))
        moved = jnp.concatenate(moved, axis=0)
        own_rows = sm[pl.ds(RAD + start, step)].reshape(step * rows, LANES)
        hi, lo = split(jnp.concatenate([own_rows, moved], axis=1))
        out = mxu(hi, yw_ref[...])
        out = out[:, :LANES] + out[:, LANES:] + mxu(lo, yw_ref[:, :LANES])
        gy[...] = out.reshape(step, rows, LANES)
        pairs = [jnp.broadcast_to(pair_ref[h], (8, LANES)) for h in range(halves)]
        colours = [jnp.broadcast_to(pal_ref[c], (8, LANES)) for c in range(4)]
        half = 0.5 * (bins - 1)
        for row in range(0, rows, 8):
            block = sm[pl.ds(start, step + 2 * RAD), row : row + 8, :]
            level = half * jnp.tanh(0.75 * block[RAD : RAD + step]) + half
            index = jnp.minimum(level.astype(jnp.int32), bins - 2)
            fraction = level - index.astype(jnp.float32)
            at = index & (LANES - 1)
            found = [lookup(pairs, at[i]) for i in range(step)]
            grad_z = slope(block, step)
            grad_x = gx[pl.ds(start, step), row : row + 8, :]
            grad_y = gy[:, row : row + 8, :]
            facing = jnp.abs(0.26726 * grad_z + 0.53452 * grad_x + 0.80178 * grad_y)
            square = jnp.maximum(grad_z * grad_z + grad_x * grad_x + grad_y * grad_y, 0.1)
            shade = 0.3 + 0.7 * facing * lax.rsqrt(square)
            low, high = [], []
            for i in range(step):
                pair = found[i][0]
                for h in range(1, halves):
                    pair = jnp.where(index[i] >= h * LANES, found[i][h], pair)
                low.append(pair & (LANES - 1))
                high.append(pair >> 7)
            first = [lookup(colours, low[i]) for i in range(step)]
            second = [lookup(colours, high[i]) for i in range(step)]
            for i in range(step):
                for c in range(4):
                    looked = first[i][c] + fraction[i] * (second[i][c] - first[i][c])
                    o_ref[c, start + i, row : row + 8, :] = looked * (shade[i] if c < 3 else factor)
        return carry

    lax.fori_loop(0, planes // step, shade_step, 0)


def second_kernel(groups, slab, blocks, haloed, *refs):
    own, refs = refs[:blocks], refs[blocks:]
    halos, refs = (refs[:2], refs[2:]) if haloed else ((), refs)
    lhs_ref, c_ref, o_ref, zin, sm, sems = refs
    copies = gather_rows(groups, slab, 0, own, halos, zin, None, sems)
    planes = zin.shape[0] - 2 * RAD
    rows = o_ref.shape[1]
    clear_ends(zin, RAD)
    for copy in copies:
        copy.wait()
    step = 8

    def march(t, carry):
        start = pl.multiple_of(t * step, step)
        stack = plane_smooth(zin, start, step)
        for q in range(0, step, 2):
            out = mxu(lhs_ref[...], jnp.concatenate([stack[q], stack[q + 1]], axis=1))
            sm[q] = out[:, :LANES]
            sm[q + 1] = out[:, LANES:]
        through, red, green, blue = carry
        for i in range(step):
            sigmoid = 0.5 * jnp.tanh(sm[i]) + 0.5
            passed = through * jnp.exp(-(c_ref[3, start + i] * sigmoid))
            weight = through - passed
            red = red + weight * c_ref[0, start + i]
            green = green + weight * c_ref[1, start + i]
            blue = blue + weight * c_ref[2, start + i]
            through = passed
        return through, red, green, blue

    zero = jnp.zeros((rows, LANES), jnp.float32)
    through, red, green, blue = lax.fori_loop(
        0, planes // step, march, (zero + 1.0, zero, zero, zero)
    )
    for c, value in enumerate((red, green, blue, through)):
        o_ref[c] = value


def vmem_call(kernel, out_shape, scratch, in_specs, name, microseconds):
    return pl.pallas_call(
        kernel,
        in_specs=in_specs,
        out_specs=pl.BlockSpec(memory_space=pltpu.VMEM),
        out_shape=jax.ShapeDtypeStruct(out_shape, jnp.float32),
        scratch_shapes=scratch,
        compiler_params=pltpu.CompilerParams(vmem_limit_bytes=40 << 20),
        cost_estimate=cost(microseconds),
        name=name,
    )


def exchange(blocks, order):
    got = [blocks[0]] + [None] * (len(blocks) - 1)
    for m in order:
        pairs = [(s, s ^ m) for s in range(len(blocks))]
        got[m] = lax.ppermute(blocks[m], GROUP, pairs)
    return got


def row_halo(blocks, groups, count, width):
    place = lax.rem(lax.axis_index(GROUP), groups)
    rows = blocks[0].shape[1]

    def of_source(which, low):
        choices = [
            jnp.stack([blocks[groups * i + g][:, low : low + width] for i in range(len(blocks) // groups)])
            for g in range(groups)
        ]
        value = choices[0]
        for g in range(1, groups):
            value = jnp.where((place ^ which) == g, choices[g], value)
        return value

    tail = of_source(groups - 1, rows - width)
    head = of_source(0, 0)
    left = lax.ppermute(tail, "strips", [(i, i + 1) for i in range(count - 1)])
    right = lax.ppermute(head, "strips", [(i + 1, i) for i in range(count - 1)])
    return left, right


def three_terms(matrix):
    hi, lo = split_np(matrix)
    return np.concatenate([hi, hi, lo], axis=1)


def local(depth, count, groups, fields, colour_palette, opacity_palette, tf_index):
    slab, strip, columns = fields.shape[1:]
    extra = slab // PER
    planes = slab * depth
    rows = strip * groups
    wide = rows + 2 * HALO
    bins = tf_index.shape[0]
    blocks = depth * groups

    bh, bl = split_np(band(S_TAPS, 2 * LANES, 4 * LANES, LANES).T)
    smooth_rows = band(S_TAPS, rows + 2 * RAD, wide, HALO - RAD)
    slope_rows = band(D_TAPS, rows, rows + 2 * RAD, RAD)
    inner = slice(HALO, rows - HALO)
    outer = np.r_[0:HALO, rows - HALO : rows]
    forms = []
    for case in range(4):
        inside = np.ones((rows + 2 * RAD, 1))
        if case & 1:
            inside[:RAD] = 0
        if case & 2:
            inside[-RAD:] = 0
        smooth, gradient = smooth_rows[RAD:-RAD], slope_rows @ (inside * smooth_rows)
        forms.append(three_terms(np.concatenate([smooth[outer], gradient[outer]], axis=0)))
        if case == 0:
            inner_form = three_terms(
                np.concatenate([smooth[inner], gradient[inner]], axis=0)[:, HALO:-HALO]
            )
    place = lax.axis_index("strips")
    case = (place == 0).astype(jnp.int32) + 2 * (place == count - 1).astype(jnp.int32)
    outer_form = lax.dynamic_index_in_dim(jnp.asarray(np.stack(forms)), case, 0, keepdims=False)
    across = np.zeros((2 * LANES, LANES))
    across[:LANES] = band(D_TAPS, LANES, LANES, 0).T
    for lane in range(LANES):
        for k in range(-RAD, RAD + 1):
            if lane + k < 0:
                across[LANES + lane + k + RAD, lane] = D_TAPS[k + RAD]
            if lane + k >= LANES:
                across[LANES + RAD + lane + k - LANES, lane] = D_TAPS[k + RAD]
    yw = np.concatenate(split_np(across), axis=1)
    zh, zl = split_np(np.kron(band(S_TAPS, PER, 3 * PER, PER).T, np.eye(2 * RAD)))

    following = jnp.concatenate([tf_index[1:], tf_index[-1:]])
    pair = (tf_index + LANES * following).reshape(bins // LANES, 1, LANES)
    palette = jnp.concatenate([colour_palette, opacity_palette[None]], axis=0)
    palette = jnp.pad(palette, ((0, 0), (0, LANES - palette.shape[1])))[:, None, :]

    anywhere = pl.BlockSpec(memory_space=pl.ANY)
    vmem = pl.BlockSpec(memory_space=pltpu.VMEM)
    f32 = jnp.float32

    def colours(own, halos, lhs, microseconds):
        mine, out = (wide, len(outer)) if halos else (rows, rows - 2 * HALO)
        return vmem_call(
            functools.partial(
                first_kernel, groups, slab, extra, blocks, bool(halos), 1.5 * (2.0 / planes)
            ),
            (4, planes, out, LANES),
            [
                pltpu.VMEM((planes + 2 * RAD, mine, LANES), f32),
                pltpu.VMEM((planes // PER + 2, mine, LANES), f32),
                pltpu.VMEM((planes + 2 * RAD, out, LANES), f32),
                pltpu.VMEM((planes, out, LANES), f32),
                pltpu.VMEM((8, out, LANES), f32),
                pltpu.VMEM((planes // PER, out, LANES), f32),
                pltpu.SemaphoreType.DMA((2 * (blocks + 2 * depth),)),
            ],
            [anywhere] * (blocks + len(halos)) + [vmem] * 6,
            "colours",
            microseconds,
        )(*own, *halos, lhs, yw, zh, zl, pair, palette)

    def march(own, halos, lhs, coloured, microseconds):
        mine, out = (wide, len(outer)) if halos else (rows, rows - 2 * HALO)
        return vmem_call(
            functools.partial(second_kernel, groups, slab, blocks, bool(halos)),
            (4, out, LANES),
            [
                pltpu.VMEM((planes + 2 * RAD, mine, LANES), f32),
                pltpu.VMEM((8, out, LANES), f32),
                pltpu.SemaphoreType.DMA((blocks + 2 * depth,)),
            ],
            [anywhere] * (blocks + len(halos)) + [vmem] * 2,
            "march",
            microseconds,
        )(*own, *halos, lhs[:out], coloured)

    order = sorted(range(1, blocks), key=lambda m: (bin(m).count("1"), m))
    sent0 = source(fields, 0, bh, bl, True)
    got0 = exchange(sent0, order)
    sent1 = source(fields, 1, bh, bl, False)
    got1 = exchange(sent1, order)
    halo0 = row_halo(got0, groups, count, HALO)
    halo1 = row_halo(got1, groups, count, HALO)
    image = []
    if rows > 2 * HALO:
        coloured = colours(got0, (), inner_form, 12)
        image.append(march(got1, (), inner_form, coloured, 5))
    coloured = colours(got0, halo0, outer_form, 12)
    image.append(march(got1, halo1, outer_form, coloured, 5))
    edge = image[-1]
    whole = jnp.concatenate([edge[:, :HALO]] + image[:-1] + [edge[:, HALO:]], axis=1)
    if groups == 1:
        return whole
    return lax.all_to_all(whole, "pair", 1, 2, tiled=True)


def solution(mesh):
    depth, tiles = mesh.devices.shape

    def program(fields, colour_palette, opacity_palette, tf_index):
        groups = max(1, fields.shape[3] // (LANES * depth))
        count = tiles // groups
        finer = Mesh(mesh.devices.reshape(depth, count, groups), ("depth", "strips", "pair"))
        return jax.shard_map(
            functools.partial(local, depth, count, groups),
            mesh=finer,
            in_specs=(P(None, "depth", ("strips", "pair"), None), P(), P(), P()),
            out_specs=P(None, ("strips", "pair"), "depth"),
            check_vma=False,
        )(fields, colour_palette, opacity_palette, tf_index)

    return program
```

```python
import functools

import jax
import jax.numpy as jnp
import ml_dtypes
import numpy as np
from jax import lax
from jax.experimental import pallas as pl
from jax.experimental.pallas import tpu as pltpu
from jax.sharding import Mesh
from jax.sharding import PartitionSpec as P


RAD = 4
LANES = 128
HALO = 8
GROUP = ("depth", "pair")
PER = LANES // (2 * RAD)

offsets = np.arange(-4.0, 5.0)
bell = np.exp(-(offsets**2) / 8.0)
S_TAPS = bell / np.sqrt(np.sum(bell**2))
slope_raw = offsets * bell
D_TAPS = slope_raw / np.sqrt(np.sum(slope_raw**2))


def split_np(matrix):
    hi = matrix.astype(ml_dtypes.bfloat16)
    lo = (matrix - hi.astype(np.float64)).astype(ml_dtypes.bfloat16)
    return hi, lo


def split(value):
    hi = value.astype(jnp.bfloat16)
    return hi, (value - hi.astype(jnp.float32)).astype(jnp.bfloat16)


def mxu(a, b):
    return jnp.dot(a, b, preferred_element_type=jnp.float32)


def band(taps, rows, cols, shift):
    matrix = np.zeros((rows, cols))
    for row in range(rows):
        for k in range(-RAD, RAD + 1):
            if 0 <= row + k + shift < cols:
                matrix[row, row + k + shift] = taps[k + RAD]
    return matrix


def symmetric(block, n):
    t = [float(x) for x in S_TAPS[RAD:]]
    out = t[0] * block[4 : 4 + n]
    for k in range(1, RAD + 1):
        out = out + t[k] * (block[4 - k : 4 - k + n] + block[4 + k : 4 + k + n])
    return out


def slope(block, n):
    t = [float(x) for x in D_TAPS[RAD:]]
    out = t[1] * (block[5 : 5 + n] - block[3 : 3 + n])
    for k in range(2, RAD + 1):
        out = out + t[k] * (block[4 + k : 4 + k + n] - block[4 - k : 4 - k + n])
    return out


def source_kernel(blocks, groups, which, edges, planes, *refs):
    fields_ref, bh_ref, bl_ref = refs[:3]
    outs, (held, us, in_sems, sems) = refs[3:-4], refs[-4:]
    if edges:
        flag_ref, outs = outs[-1], outs[:-1]
    joined = len(outs) == blocks
    slab, rows, columns = held.shape
    steps = slab // planes
    wide = 2 * LANES

    def fetch(step):
        part = pl.ds(step * planes, planes)
        return pltpu.make_async_copy(fields_ref.at[which, part], held.at[part], in_sems.at[step])

    for step in range(steps):
        fetch(step).start()

    def filtered(step):
        values = held[pl.ds(step * planes, planes)].reshape(planes * rows, columns)
        hi, lo = split(values)
        for j in range(columns // wide):
            left, right = max(0, wide * j - LANES), min(columns, wide * (j + 1) + LANES)
            base = left - (wide * j - LANES)
            bh = bh_ref[base : base + right - left]
            bl = bl_ref[base : base + right - left]
            u = mxu(hi[:, left:right], bh) + mxu(lo[:, left:right], bh) + mxu(hi[:, left:right], bl)
            for h in range(2):
                us[2 * j + h, pl.ds(step * planes, planes)] = u[
                    :, h * LANES : (h + 1) * LANES
                ].reshape(planes, rows, LANES)

    me = lax.axis_index(GROUP)
    place = lax.rem(me, groups)

    if edges:
        flag_ref[...] = jnp.zeros(flag_ref.shape, jnp.float32) + (place == groups - 1).astype(jnp.float32)

    def copies(at, first, count):
        found = []
        for m in range(blocks):
            for h in range(2):
                row = pl.multiple_of(HALO * (h ^ place), HALO)
                target = outs[m].at[h] if joined else outs[h * blocks + m]
                found.append(
                    pltpu.make_async_copy(
                        us.at[me ^ m, pl.ds(first, count), pl.ds(row, HALO)],
                        target.at[pl.ds(first, count)],
                        sems.at[at, 2 * m + h],
                    )
                )
        return found

    def collected(step):
        lane = lax.broadcasted_iota(jnp.int32, (rows, LANES), 1)
        zero = jnp.zeros((rows, LANES), jnp.float32)
        part = lax.rem(step, PER // planes) * planes
        at = slab + step * planes // PER
        for b in range(blocks):
            acc = us[b, at]
            for z in range(planes):
                before = us[b - 1, step * planes + z] if b > 0 else zero
                after = us[b + 1, step * planes + z] if b < blocks - 1 else zero
                both = jnp.where(lane >= LANES // 2, before, after)
                moved = pltpu.roll(both, lax.rem(RAD + 2 * RAD * (z + part), LANES), 1)
                acc = jnp.where(lane // (2 * RAD) == z + part, moved, acc)
            us[b, at] = acc

    def body(step, carry):
        fetch(step).wait()
        filtered(step)
        for copy in copies(step, step * planes, planes):
            copy.start()
        if edges:
            collected(step)
        return carry

    lax.fori_loop(0, steps, body, 0)
    last = copies(steps, slab, edges) if edges else []
    for copy in last:
        copy.start()
    for at in range(steps):
        for copy in copies(at, at * planes, planes):
            copy.wait()
    for copy in last:
        copy.wait()


def source(fields, which, groups, bh, bl, edges, joined, vmem):
    _, slab, rows, columns = fields.shape
    blocks = columns // LANES
    extra = slab // PER if edges else 0
    planes = 8
    steps = slab // planes
    block = (slab + extra, HALO, LANES)
    shapes = [(2,) + block] * blocks if joined else [block] * (2 * blocks)
    flag_spec = [pl.BlockSpec(memory_space=pltpu.VMEM)] if edges else []
    flag_shape = [(8, LANES)] if edges else []
    return pl.pallas_call(
        functools.partial(source_kernel, blocks, groups, which, extra, planes),
        in_specs=[pl.BlockSpec(memory_space=pltpu.HBM)] + [pl.BlockSpec(memory_space=pltpu.VMEM)] * 2,
        out_specs=[pl.BlockSpec(memory_space=pl.ANY)] * len(shapes) + flag_spec,
        out_shape=[jax.ShapeDtypeStruct(shape, jnp.float32) for shape in shapes + flag_shape],
        scratch_shapes=[
            pltpu.VMEM((slab, rows, columns), jnp.float32),
            pltpu.VMEM((blocks, slab + extra, rows, LANES), jnp.float32),
            pltpu.SemaphoreType.DMA((steps,)),
            pltpu.SemaphoreType.DMA((steps + 1, 2 * blocks)),
        ],
        compiler_params=pltpu.CompilerParams(vmem_limit_bytes=vmem),
        cost_estimate=cost(5),
        name="columns_filter",
    )(fields, bh, bl)


def cost(microseconds):
    return pl.CostEstimate(flops=0, bytes_accessed=int(microseconds * 3e6), transcendentals=0)


def gather_rows(groups, slab, extra, own, halos, zin, ein, sems):
    me = lax.axis_index(GROUP)
    first = HALO if halos else 0
    parts = []
    joined = len(own[0].shape) == 4
    blocks = len(own) if joined else len(own) // 2
    for m in range(blocks):
        d, g = (me ^ m) // groups, lax.rem(me ^ m, groups)
        for h in range(2):
            ref = own[m].at[h] if joined else own[h * blocks + m]
            parts.append((ref, d, first + HALO * (2 * g + (h ^ g))))
    end = zin.shape[1] - HALO
    leads = lax.rem(me, groups) == groups - 1
    narrow = halos and halos[0].shape[2] < HALO
    if halos and not narrow:
        for i in range(halos[0].shape[0]):
            d = (me // groups) ^ i
            parts.append((halos[0].at[i], d, jnp.where(leads, 0, end)))
            parts.append((halos[1].at[i], d, jnp.where(leads, end, 0)))
    copies = []
    for ref, d, row in parts:
        row = pl.multiple_of(row, HALO)
        copies.append(
            pltpu.make_async_copy(
                ref.at[pl.ds(0, slab)],
                zin.at[pl.ds(RAD + d * slab, slab), pl.ds(row, HALO)],
                sems.at[len(copies)],
            )
        )
        if extra:
            copies.append(
                pltpu.make_async_copy(
                    ref.at[pl.ds(slab, extra)],
                    ein.at[pl.ds(1 + d * extra, extra), pl.ds(row, HALO)],
                    sems.at[len(copies)],
                )
            )
    for copy in copies:
        copy.start()
    if narrow:
        for i in range(halos[0].shape[0]):
            part = pl.ds(RAD + ((me // groups) ^ i) * slab, slab)
            one, other = halos[0][i], halos[1][i]
            zin[part, HALO - RAD : HALO, :] = jnp.where(leads, one, other)
            zin[part, end : end + RAD, :] = jnp.where(leads, other, one)
    return copies


def clear_ends(ref, width):
    zero = jnp.zeros((width,) + ref.shape[1:], jnp.float32)
    ref[:width] = zero
    ref[ref.shape[0] - width :] = zero


def plane_smooth(zin, start, count):
    tiles = []
    for row in range(0, zin.shape[1], 8):
        tiles.append(symmetric(zin[pl.ds(start, count + 2 * RAD), row : row + 8, :], count))
    hi, lo = split(jnp.concatenate(tiles, axis=1))
    return jnp.concatenate([hi, lo, hi], axis=1)


def lookup(tables, index):
    return [jnp.take_along_axis(t, index, axis=1, mode="promise_in_bounds") for t in tables]


def first_kernel(groups, slab, extra, blocks, count_strips, factor, *refs):
    own, halos, refs = refs[: 2 * blocks], refs[2 * blocks : 2 * blocks + 2], refs[2 * blocks + 2 :]
    lhs_ref, yw_ref, zh_ref, zl_ref, pair_ref, pal_ref = refs[:6]
    outs = refs[6:-9]
    zin, ein, sm, gx, gy, es, found_ref, fraction_ref, sems = refs[-9:]
    copies = gather_rows(groups, slab, extra, own, halos, zin, ein, sems)
    planes = zin.shape[0] - 2 * RAD
    rows = sm.shape[1]
    wide = zin.shape[1]
    place = lax.axis_index("strips")
    case = (place == 0).astype(jnp.int32) + 2 * (place == count_strips - 1).astype(jnp.int32)
    lhs_ref = lhs_ref.at[case]
    clear_ends(zin, RAD)
    clear_ends(sm, RAD)
    clear_ends(ein, 1)
    for copy in copies:
        copy.wait()
    step = 8

    near = [ein[j] for j in range(ein.shape[0])]
    count = len(near) - 2
    stacked = jnp.concatenate(
        [jnp.concatenate(near[k : k + count], axis=0) for k in range(3)], axis=1
    )
    hi, lo = split(stacked)
    ez = mxu(hi, zh_ref[...]) + mxu(lo, zh_ref[...]) + mxu(hi, zl_ref[...])
    hi, lo = split(ez.reshape(count, wide, LANES))
    stack = jnp.concatenate([hi, lo, hi], axis=1)
    for j in range(0, count, 2):
        out = mxu(lhs_ref[:rows], jnp.concatenate([stack[j], stack[j + 1]], axis=1))
        es[j] = out[:, :LANES]
        es[j + 1] = out[:, LANES:]

    def smooth_stage(t):
        start = pl.multiple_of(t * step, step)
        stack = plane_smooth(zin, start, step)
        for q in range(0, step, 2):
            out = mxu(lhs_ref[...], jnp.concatenate([stack[q], stack[q + 1]], axis=1))
            for h in range(2):
                part = out[:, h * LANES : (h + 1) * LANES]
                sm[RAD + start + q + h] = part[:rows]
                gx[start + q + h] = part[rows:]

    def across_stage(t):
        start = pl.multiple_of(t * step, step)
        group = es[start // PER]
        moved = []
        for i in range(step):
            shift = (LANES - 2 * RAD * (lax.rem(start, PER) + i)) % LANES
            moved.append(pltpu.roll(group, shift, 1))
        moved = jnp.concatenate(moved, axis=0)
        own_rows = sm[pl.ds(RAD + start, step)].reshape(step * rows, LANES)
        hi, lo = split(jnp.concatenate([own_rows, moved], axis=1))
        out = mxu(hi, yw_ref[...])
        out = out[:, :LANES] + out[:, LANES:] + mxu(lo, yw_ref[:, :LANES])
        gy[pl.ds(start, step)] = out.reshape(step, rows, LANES)

    halves = pair_ref.shape[0]
    bins = halves * LANES
    half = 0.5 * (bins - 1)

    def index_stage(t):
        start = pl.multiple_of(t * step, step)
        pairs = [jnp.broadcast_to(pair_ref[h], (8, LANES)) for h in range(halves)]
        for row in range(0, rows, 8):
            level = half * jnp.tanh(0.75 * sm[pl.ds(RAD + start, step), row : row + 8, :]) + half
            index = jnp.minimum(level.astype(jnp.int32), bins - 2)
            fraction_ref[t & 1, :, row : row + 8, :] = level - index.astype(jnp.float32)
            at = index & (LANES - 1)
            found = [lookup(pairs, at[i]) for i in range(step)]
            for i in range(step):
                pair = found[i][0]
                for h in range(1, halves):
                    pair = jnp.where(index[i] >= h * LANES, found[i][h], pair)
                found_ref[t & 1, i, row : row + 8, :] = pair

    def colour_stage(t):
        start = pl.multiple_of(t * step, step)
        colours = [jnp.broadcast_to(pal_ref[c], (8, LANES)) for c in range(4)]
        for row in range(0, rows, 8):
            if row == 0 or row == rows - 8:
                o_ref, at = outs[0], min(row, 8)
            else:
                o_ref, at = outs[1], row - 8
            pair = found_ref[t & 1, :, row : row + 8, :]
            fraction = fraction_ref[t & 1, :, row : row + 8, :]
            low, high = pair & (LANES - 1), pair >> 7
            first = [lookup(colours, low[i]) for i in range(step)]
            second = [lookup(colours, high[i]) for i in range(step)]
            grad_z = slope(sm[pl.ds(start, step + 2 * RAD), row : row + 8, :], step)
            grad_x = gx[pl.ds(start, step), row : row + 8, :]
            grad_y = gy[pl.ds(start, step), row : row + 8, :]
            facing = jnp.abs(0.26726 * grad_z + 0.53452 * grad_x + 0.80178 * grad_y)
            square = jnp.maximum(grad_z * grad_z + grad_x * grad_x + grad_y * grad_y, 0.1)
            shade = 0.3 + 0.7 * facing * lax.rsqrt(square)
            for i in range(step):
                for c in range(4):
                    looked = first[i][c] + fraction[i] * (second[i][c] - first[i][c])
                    o_ref[c, start + i, at : at + 8, :] = looked * (shade[i] if c < 3 else factor)

    steps = planes // step
    smooth_stage(0)
    index_stage(0)
    across_stage(0)
    smooth_stage(1)

    def body(t, carry):
        colour_stage(t - 2)
        index_stage(t - 1)
        across_stage(t - 1)
        smooth_stage(t)
        return carry

    lax.fori_loop(2, steps, body, 0)
    colour_stage(steps - 2)
    index_stage(steps - 1)
    across_stage(steps - 1)
    colour_stage(steps - 1)


def second_kernel(groups, slab, blocks, haloed, joins, *refs):
    own, refs = refs[:blocks], refs[blocks:]
    halos, refs = (refs[:2], refs[2:]) if haloed else ((), refs)
    (lhs_ref, c_ref), (zin, sm, sems) = refs[:2], refs[-3:]
    image_ref, outs = (refs[2], refs[3:-3]) if joins else (None, refs[2:-3])
    copies = gather_rows(groups, slab, 0, own, halos, zin, None, sems)
    planes = zin.shape[0] - 2 * RAD
    rows = sm.shape[1]
    step = 8

    clear_ends(zin, RAD)
    for copy in copies:
        copy.wait()

    def march(t, carry):
        start = pl.multiple_of(t * step, step)
        stack = plane_smooth(zin, start, step)
        for q in range(0, step, 2):
            out = mxu(lhs_ref[...], jnp.concatenate([stack[q], stack[q + 1]], axis=1))
            sm[q] = out[:, :LANES]
            sm[q + 1] = out[:, LANES:]
        through, red, green, blue = carry
        for i in range(step):
            sigmoid = 0.5 * jnp.tanh(sm[i]) + 0.5
            passed = through * jnp.exp(-(c_ref[3, start + i] * sigmoid))
            weight = through - passed
            red = red + weight * c_ref[0, start + i]
            green = green + weight * c_ref[1, start + i]
            blue = blue + weight * c_ref[2, start + i]
            through = passed
        return through, red, green, blue

    zero = jnp.zeros((rows, LANES), jnp.float32)
    through, red, green, blue = lax.fori_loop(
        0, planes // step, march, (zero + 1.0, zero, zero, zero)
    )
    first = lax.rem(lax.axis_index(GROUP), groups) == 0
    for c, value in enumerate((red, green, blue, through)):
        if joins:
            strips = (
                jnp.concatenate([value[:8], image_ref[c, :8]], axis=0),
                jnp.concatenate([image_ref[c, 8:], value[8:]], axis=0),
            )
            outs[0][c] = jnp.where(first, strips[0], strips[1])
            outs[1][c] = jnp.where(first, strips[1], strips[0])
        else:
            outs[0][c] = value


def vmem_call(kernel, shapes, scratch, in_specs, microseconds, limit):
    return pl.pallas_call(
        kernel,
        in_specs=in_specs,
        out_specs=[pl.BlockSpec(memory_space=pltpu.VMEM)] * len(shapes),
        out_shape=[jax.ShapeDtypeStruct(shape, jnp.float32) for shape in shapes],
        scratch_shapes=scratch,
        compiler_params=pltpu.CompilerParams(vmem_limit_bytes=limit << 20),
        cost_estimate=cost(microseconds),
    )


def exchange(blocks, order):
    blocks = list(blocks)
    got = blocks[:1] + [None] * (len(blocks) - 1)
    for m in order:
        pairs = [(s, s ^ m) for s in range(len(blocks))]
        got[m] = lax.ppermute(blocks[m], GROUP, pairs)
    return got


def row_halo(blocks, groups, count, leads):
    joined = blocks[0].ndim == 4
    total = len(blocks) if joined else len(blocks) // 2
    found = []
    for which in range(2):
        half, member = (0, which) if groups > 1 else (1 - which, 0)
        edge = []
        for i in range(total // groups):
            m = groups * i + member
            if joined:
                low, high = blocks[m][half, :, :RAD], blocks[m][half, :, HALO - RAD :]
                edge.append(jnp.where(leads, low, high) if which else jnp.where(leads, high, low))
            else:
                edge.append(blocks[half * total + m])
        pairs = []
        for strip in range(count):
            for g in range(groups):
                other = strip + (1 if (g == groups - 1) == (which == 0) else -1)
                if 0 <= other < count:
                    pairs.append((strip * groups + g, other * groups + g))
        found.append(lax.ppermute(jnp.stack(edge), ("strips", "pair"), pairs))
    return found


def three_terms(matrix):
    hi, lo = split_np(matrix)
    return np.concatenate([hi, hi, lo], axis=1)


def local(depth, count, groups, fields, colour_palette, opacity_palette, tf_index):
    slab, strip, _ = fields.shape[1:]
    extra = slab // PER
    planes = slab * depth
    rows = strip * groups
    wide = rows + 2 * HALO
    bins = tf_index.shape[0]
    blocks = depth * groups

    bh, bl = split_np(band(S_TAPS, 2 * LANES, 4 * LANES, LANES).T)
    smooth_rows = band(S_TAPS, rows + 2 * RAD, wide, HALO - RAD)
    slope_rows = band(D_TAPS, rows, rows + 2 * RAD, RAD)
    inner = slice(HALO, rows - HALO)
    outer = np.r_[0:HALO, rows - HALO : rows]
    forms = []
    for case in range(4):
        inside = np.ones((rows + 2 * RAD, 1))
        if case & 1:
            inside[:RAD] = 0
        if case & 2:
            inside[-RAD:] = 0
        smooth, gradient = smooth_rows[RAD:-RAD], slope_rows @ (inside * smooth_rows)
        forms.append(three_terms(np.concatenate([smooth, gradient], axis=0)))
    edge_form = three_terms(smooth[outer])
    inner_form = three_terms(smooth[inner][:, HALO:-HALO])
    form = jnp.asarray(np.stack(forms))
    across = np.zeros((2 * LANES, LANES))
    across[:LANES] = band(D_TAPS, LANES, LANES, 0).T
    for lane in range(LANES):
        for k in range(-RAD, RAD + 1):
            if lane + k < 0:
                across[LANES + lane + k + RAD, lane] = D_TAPS[k + RAD]
            if lane + k >= LANES:
                across[LANES + RAD + lane + k - LANES, lane] = D_TAPS[k + RAD]
    yw = np.concatenate(split_np(across), axis=1)
    zh, zl = split_np(np.kron(band(S_TAPS, PER, 3 * PER, PER).T, np.eye(2 * RAD)))

    following = jnp.concatenate([tf_index[1:], tf_index[-1:]])
    pair = (tf_index + LANES * following).reshape(bins // LANES, 1, LANES)
    palette = jnp.concatenate([colour_palette, opacity_palette[None]], axis=0)
    palette = jnp.pad(palette, ((0, 0), (0, LANES - palette.shape[1])))[:, None, :]

    anywhere = pl.BlockSpec(memory_space=pl.ANY)
    vmem = pl.BlockSpec(memory_space=pltpu.VMEM)
    f32 = jnp.float32

    def colours(own, halos, lhs):
        shapes = [(4, planes, len(outer), LANES)]
        if rows > len(outer):
            shapes.append((4, planes, rows - len(outer), LANES))
        return vmem_call(
            functools.partial(first_kernel, groups, slab, extra, blocks, count, 1.5 * (2.0 / planes)),
            shapes,
            [
                pltpu.VMEM((planes + 2 * RAD, wide, LANES), f32),
                pltpu.VMEM((planes // PER + 2, wide, LANES), f32),
                pltpu.VMEM((planes + 2 * RAD, rows, LANES), f32),
                pltpu.VMEM((planes, rows, LANES), f32),
                pltpu.VMEM((planes, rows, LANES), f32),
                pltpu.VMEM((planes // PER, rows, LANES), f32),
                pltpu.VMEM((2, 8, rows, LANES), jnp.int32),
                pltpu.VMEM((2, 8, rows, LANES), f32),
                pltpu.SemaphoreType.DMA((4 * (blocks + depth),)),
            ],
            [anywhere] * (2 * blocks + 2) + [vmem] * 6,
            20,
            16,
        )(*own, *halos, lhs, yw, zh, zl, pair, palette)

    def march(own, halos, lhs, coloured, *others):
        mine, out = (wide, len(outer)) if halos else (rows, rows - len(outer))
        return vmem_call(
            functools.partial(second_kernel, groups, slab, blocks, bool(halos), bool(others)),
            [(4, out, LANES)] * (1 + len(others)),
            [
                pltpu.VMEM((planes + 2 * RAD, mine, LANES), f32),
                pltpu.VMEM((8, out, LANES), f32),
                pltpu.SemaphoreType.DMA((2 * blocks,)),
            ],
            [anywhere] * blocks + [vmem] * (len(halos) + 2 + len(others)),
            5,
            10,
        )(*own, *halos, lhs, coloured, *others)

    order = sorted(range(1, blocks), key=lambda m: (bin(m).count("1"), m))
    sent0 = list(source(fields, 0, groups, bh, bl, True, False, 60 << 20))
    leads = sent0.pop()[0] > 0.5
    got0 = exchange(sent0[:blocks], order) + exchange(sent0[blocks:], order)
    bh, pair, palette = lax.optimization_barrier((jnp.asarray(bh), pair, palette))
    sent1 = source(fields, 1, groups, bh, bl, False, True, 16 << 20)
    halo0 = row_halo(got0, groups, count, leads)
    got1 = exchange(sent1, order)
    halo1 = row_halo(got1, groups, count, leads)
    coloured = colours(got0, halo0, form)
    others = ()
    if rows > len(outer):
        others = march(got1, (), inner_form, coloured[1])
    image = march(got1, halo1, edge_form, coloured[0], *others)
    if groups == 1:
        return image[0]
    given = lax.ppermute(image[1], "pair", [(0, 1), (1, 0)])
    return jnp.concatenate(
        [jnp.where(leads, given, image[0]), jnp.where(leads, image[0], given)], axis=2
    )


def solution(mesh):
    depth, tiles = mesh.devices.shape

    def program(fields, colour_palette, opacity_palette, tf_index):
        groups = max(1, fields.shape[3] // (LANES * depth))
        count = tiles // groups
        finer = Mesh(mesh.devices.reshape(depth, count, groups), ("depth", "strips", "pair"))

        def body(*arrays):
            return local(depth, count, groups, *arrays)

        mapped = jax.shard_map(
            body,
            mesh=finer,
            in_specs=(P(None, "depth", ("strips", "pair"), None), P(), P(), P()),
            out_specs=P(None, ("strips", "pair"), "depth"),
            check_vma=False,
        )
        return mapped(fields, colour_palette, opacity_palette, tf_index)

    return program
```

```python
import functools

import jax
import jax.numpy as jnp
import ml_dtypes
import numpy as np
from jax import lax
from jax.experimental import pallas as pl
from jax.experimental.pallas import tpu as pltpu
from jax.sharding import Mesh
from jax.sharding import PartitionSpec as P


RAD = 4
LANES = 128
HALO = 8
GROUP = ("depth", "pair")
PER = LANES // (2 * RAD)

offsets = np.arange(-4.0, 5.0)
bell = np.exp(-(offsets**2) / 8.0)
S_TAPS = bell / np.sqrt(np.sum(bell**2))
slope_raw = offsets * bell
D_TAPS = slope_raw / np.sqrt(np.sum(slope_raw**2))


def split_np(matrix):
    hi = matrix.astype(ml_dtypes.bfloat16)
    lo = (matrix - hi.astype(np.float64)).astype(ml_dtypes.bfloat16)
    return hi, lo


def split(value):
    hi = value.astype(jnp.bfloat16)
    return hi, (value - hi.astype(jnp.float32)).astype(jnp.bfloat16)


def mxu(a, b):
    return jnp.dot(a, b, preferred_element_type=jnp.float32)


def band(taps, rows, cols, shift):
    matrix = np.zeros((rows, cols))
    for row in range(rows):
        for k in range(-RAD, RAD + 1):
            if 0 <= row + k + shift < cols:
                matrix[row, row + k + shift] = taps[k + RAD]
    return matrix


def symmetric(block, n):
    t = [float(x) for x in S_TAPS[RAD:]]
    out = t[0] * block[4 : 4 + n]
    for k in range(1, RAD + 1):
        out = out + t[k] * (block[4 - k : 4 - k + n] + block[4 + k : 4 + k + n])
    return out


def slope(block, n):
    t = [float(x) for x in D_TAPS[RAD:]]
    out = t[1] * (block[5 : 5 + n] - block[3 : 3 + n])
    for k in range(2, RAD + 1):
        out = out + t[k] * (block[4 + k : 4 + k + n] - block[4 - k : 4 - k + n])
    return out


def source_kernel(blocks, groups, which, edges, planes, *refs):
    fields_ref, bands_ref = refs[:2]
    outs, (held, bands, us, ev, in_sems, sems) = refs[2:-6], refs[-6:]
    if edges:
        flag_ref, outs = outs[-1], outs[:-1]
    joined = len(outs) == blocks
    slab, rows, columns = held.shape
    steps = slab // planes
    wide = 2 * LANES

    def fetch(step):
        part = pl.ds(step * planes, planes)
        return pltpu.make_async_copy(fields_ref.at[which, part], held.at[part], in_sems.at[step])

    matrices = pltpu.make_async_copy(bands_ref, bands, in_sems.at[steps])
    fetch(0).start()
    matrices.start()
    for step in range(1, steps):
        fetch(step).start()

    def filtered(step):
        values = held[pl.ds(step * planes, planes)].reshape(planes * rows, columns)
        hi, lo = split(values)
        for j in range(columns // wide):
            left, right = max(0, wide * j - LANES), min(columns, wide * (j + 1) + LANES)
            base = left - (wide * j - LANES)
            bh = bands[0, base : base + right - left]
            bl = bands[1, base : base + right - left]
            u = mxu(hi[:, left:right], bh) + mxu(lo[:, left:right], bh) + mxu(hi[:, left:right], bl)
            for h in range(2):
                us[2 * j + h, pl.ds(step * planes, planes)] = u[
                    :, h * LANES : (h + 1) * LANES
                ].reshape(planes, rows, LANES)

    me = lax.axis_index(GROUP)
    place = lax.rem(me, groups)

    if edges:
        flag_ref[...] = jnp.zeros(flag_ref.shape, jnp.float32) + (place == groups - 1).astype(jnp.float32)

    def copies(at, origin, start, first, count):
        found = []
        for m in range(blocks):
            for h in range(2):
                row = pl.multiple_of(HALO * (h ^ place), HALO)
                target = outs[m].at[h] if joined else outs[h * blocks + m]
                found.append(
                    pltpu.make_async_copy(
                        origin.at[me ^ m, pl.ds(start, count), pl.ds(row, HALO)],
                        target.at[pl.ds(first, count)],
                        sems.at[at, 2 * m + h],
                    )
                )
        return found

    def collected(step):
        lane = lax.broadcasted_iota(jnp.int32, (rows, LANES), 1)
        zero = jnp.zeros((rows, LANES), jnp.float32)
        part = lax.rem(step, PER // planes) * planes
        at = step * planes // PER
        for b in range(blocks):
            acc = ev[b, at]
            for z in range(planes):
                before = us[b - 1, step * planes + z] if b > 0 else zero
                after = us[b + 1, step * planes + z] if b < blocks - 1 else zero
                both = jnp.where(lane >= LANES // 2, before, after)
                moved = pltpu.roll(both, lax.rem(RAD + 2 * RAD * (z + part), LANES), 1)
                acc = jnp.where(lane // (2 * RAD) == z + part, moved, acc)
            ev[b, at] = acc

    def body(step, carry):
        fetch(step).wait()
        filtered(step)
        for copy in copies(step, us, step * planes, step * planes, planes):
            copy.start()
        if edges:
            collected(step)
        return carry

    matrices.wait()
    lax.fori_loop(0, steps, body, 0)
    last = copies(steps, ev, 0, slab, edges) if edges else []
    for copy in last:
        copy.start()
    for at in range(steps):
        for copy in copies(at, us, at * planes, at * planes, planes):
            copy.wait()
    for copy in last:
        copy.wait()


def source(fields, which, groups, bands, edges, joined, vmem):
    _, slab, rows, columns = fields.shape
    blocks = columns // LANES
    extra = slab // PER if edges else 0
    planes = 8
    steps = slab // planes
    block = (slab + extra, HALO, LANES)
    shapes = [(2,) + block] * blocks if joined else [block] * (2 * blocks)
    flag_spec = [pl.BlockSpec(memory_space=pltpu.VMEM)] if edges else []
    flag_shape = [(8, LANES)] if edges else []
    return pl.pallas_call(
        functools.partial(source_kernel, blocks, groups, which, extra, planes),
        in_specs=[pl.BlockSpec(memory_space=pltpu.HBM)] * 2,
        out_specs=[pl.BlockSpec(memory_space=pl.ANY)] * len(shapes) + flag_spec,
        out_shape=[jax.ShapeDtypeStruct(shape, jnp.float32) for shape in shapes + flag_shape],
        scratch_shapes=[
            pltpu.VMEM((slab, rows, columns), jnp.float32),
            pltpu.VMEM(bands.shape, jnp.bfloat16),
            pltpu.VMEM((blocks, slab, rows, LANES), jnp.float32),
            pltpu.VMEM((blocks, max(extra, 1), rows, LANES), jnp.float32),
            pltpu.SemaphoreType.DMA((steps + 1,)),
            pltpu.SemaphoreType.DMA((steps + 1, 2 * blocks)),
        ],
        compiler_params=pltpu.CompilerParams(vmem_limit_bytes=vmem),
        cost_estimate=cost(5),
        name="columns_filter",
    )(fields, bands)


def cost(microseconds):
    return pl.CostEstimate(flops=0, bytes_accessed=int(microseconds * 3e6), transcendentals=0)


def gather_rows(groups, slab, extra, own, halos, zin, ein, sems):
    me = lax.axis_index(GROUP)
    first = HALO if halos else 0
    parts = []
    joined = len(own[0].shape) == 4
    blocks = len(own) if joined else len(own) // 2
    for m in range(blocks):
        d, g = (me ^ m) // groups, lax.rem(me ^ m, groups)
        for h in range(2):
            ref = own[m].at[h] if joined else own[h * blocks + m]
            parts.append((ref, d, first + HALO * (2 * g + (h ^ g))))
    end = zin.shape[1] - HALO
    leads = lax.rem(me, groups) == groups - 1
    narrow = halos and halos[0].shape[2] < HALO
    if halos and not narrow:
        for i in range(halos[0].shape[0]):
            d = (me // groups) ^ i
            parts.append((halos[0].at[i], d, jnp.where(leads, 0, end)))
            parts.append((halos[1].at[i], d, jnp.where(leads, end, 0)))
    copies = []
    for ref, d, row in parts:
        row = pl.multiple_of(row, HALO)
        copies.append(
            pltpu.make_async_copy(
                ref.at[pl.ds(0, slab)],
                zin.at[pl.ds(RAD + d * slab, slab), pl.ds(row, HALO)],
                sems.at[len(copies)],
            )
        )
        if extra:
            copies.append(
                pltpu.make_async_copy(
                    ref.at[pl.ds(slab, extra)],
                    ein.at[pl.ds(1 + d * extra, extra), pl.ds(row, HALO)],
                    sems.at[len(copies)],
                )
            )
    for copy in copies:
        copy.start()
    if narrow:
        for i in range(halos[0].shape[0]):
            part = pl.ds(RAD + ((me // groups) ^ i) * slab, slab)
            one, other = halos[0][i], halos[1][i]
            zin[part, HALO - RAD : HALO, :] = jnp.where(leads, one, other)
            zin[part, end : end + RAD, :] = jnp.where(leads, other, one)
    return copies


def clear_ends(ref, width):
    zero = jnp.zeros((width,) + ref.shape[1:], jnp.float32)
    ref[:width] = zero
    ref[ref.shape[0] - width :] = zero


def plane_smooth(zin, start, count):
    tiles = []
    for row in range(0, zin.shape[1], 8):
        tiles.append(symmetric(zin[pl.ds(start, count + 2 * RAD), row : row + 8, :], count))
    hi, lo = split(jnp.concatenate(tiles, axis=1))
    return jnp.concatenate([hi, lo, hi], axis=1)


def lookup(tables, index):
    return [jnp.take_along_axis(t, index, axis=1, mode="promise_in_bounds") for t in tables]


def first_kernel(groups, slab, extra, blocks, count_strips, factor, *refs):
    own, halos, refs = refs[: 2 * blocks], refs[2 * blocks : 2 * blocks + 2], refs[2 * blocks + 2 :]
    lhs_ref, yw_ref, zh_ref, zl_ref, pair_ref, pal_ref = refs[:6]
    outs = refs[6:-9]
    zin, ein, sm, gx, gy, es, found_ref, fraction_ref, sems = refs[-9:]
    copies = gather_rows(groups, slab, extra, own, halos, zin, ein, sems)
    planes = zin.shape[0] - 2 * RAD
    rows = sm.shape[1]
    wide = zin.shape[1]
    place = lax.axis_index("strips")
    case = (place == 0).astype(jnp.int32) + 2 * (place == count_strips - 1).astype(jnp.int32)
    lhs_ref = lhs_ref.at[case]
    clear_ends(zin, RAD)
    clear_ends(sm, RAD)
    clear_ends(ein, 1)
    for copy in copies:
        copy.wait()
    step = 8

    near = [ein[j] for j in range(ein.shape[0])]
    count = len(near) - 2
    stacked = jnp.concatenate(
        [jnp.concatenate(near[k : k + count], axis=0) for k in range(3)], axis=1
    )
    hi, lo = split(stacked)
    ez = mxu(hi, zh_ref[...]) + mxu(lo, zh_ref[...]) + mxu(hi, zl_ref[...])
    hi, lo = split(ez.reshape(count, wide, LANES))
    stack = jnp.concatenate([hi, lo, hi], axis=1)
    for j in range(0, count, 2):
        out = mxu(lhs_ref[:rows], jnp.concatenate([stack[j], stack[j + 1]], axis=1))
        es[j] = out[:, :LANES]
        es[j + 1] = out[:, LANES:]

    def smooth_stage(t):
        start = pl.multiple_of(t * step, step)
        stack = plane_smooth(zin, start, step)
        for q in range(0, step, 2):
            out = mxu(lhs_ref[...], jnp.concatenate([stack[q], stack[q + 1]], axis=1))
            for h in range(2):
                part = out[:, h * LANES : (h + 1) * LANES]
                sm[RAD + start + q + h] = part[:rows]
                gx[start + q + h] = part[rows:]

    def across_stage(t):
        start = pl.multiple_of(t * step, step)
        group = es[start // PER]
        moved = []
        for i in range(step):
            shift = (LANES - 2 * RAD * (lax.rem(start, PER) + i)) % LANES
            moved.append(pltpu.roll(group, shift, 1))
        moved = jnp.concatenate(moved, axis=0)
        own_rows = sm[pl.ds(RAD + start, step)].reshape(step * rows, LANES)
        hi, lo = split(jnp.concatenate([own_rows, moved], axis=1))
        out = mxu(hi, yw_ref[...])
        out = out[:, :LANES] + out[:, LANES:] + mxu(lo, yw_ref[:, :LANES])
        gy[pl.ds(start, step)] = out.reshape(step, rows, LANES)

    halves = pair_ref.shape[0]
    bins = halves * LANES
    half = 0.5 * (bins - 1)

    def index_stage(t):
        start = pl.multiple_of(t * step, step)
        pairs = [jnp.broadcast_to(pair_ref[h], (8, LANES)) for h in range(halves)]
        for row in range(0, rows, 8):
            level = half * jnp.tanh(0.75 * sm[pl.ds(RAD + start, step), row : row + 8, :]) + half
            index = jnp.minimum(level.astype(jnp.int32), bins - 2)
            fraction_ref[t & 1, :, row : row + 8, :] = level - index.astype(jnp.float32)
            at = index & (LANES - 1)
            found = [lookup(pairs, at[i]) for i in range(step)]
            for i in range(step):
                pair = found[i][0]
                for h in range(1, halves):
                    pair = jnp.where(index[i] >= h * LANES, found[i][h], pair)
                found_ref[t & 1, i, row : row + 8, :] = pair

    def colour_stage(t):
        start = pl.multiple_of(t * step, step)
        colours = [jnp.broadcast_to(pal_ref[c], (8, LANES)) for c in range(4)]
        for row in range(0, rows, 8):
            if row == 0 or row == rows - 8:
                o_ref, at = outs[0], min(row, 8)
            else:
                o_ref, at = outs[1], row - 8
            pair = found_ref[t & 1, :, row : row + 8, :]
            fraction = fraction_ref[t & 1, :, row : row + 8, :]
            low, high = pair & (LANES - 1), pair >> 7
            first = [lookup(colours, low[i]) for i in range(step)]
            second = [lookup(colours, high[i]) for i in range(step)]
            grad_z = slope(sm[pl.ds(start, step + 2 * RAD), row : row + 8, :], step)
            grad_x = gx[pl.ds(start, step), row : row + 8, :]
            grad_y = gy[pl.ds(start, step), row : row + 8, :]
            facing = jnp.abs(0.26726 * grad_z + 0.53452 * grad_x + 0.80178 * grad_y)
            square = jnp.maximum(grad_z * grad_z + grad_x * grad_x + grad_y * grad_y, 0.1)
            shade = 0.3 + 0.7 * facing * lax.rsqrt(square)
            for i in range(step):
                for c in range(4):
                    looked = first[i][c] + fraction[i] * (second[i][c] - first[i][c])
                    o_ref[c, start + i, at : at + 8, :] = looked * (shade[i] if c < 3 else factor)

    steps = planes // step
    smooth_stage(0)
    index_stage(0)
    across_stage(0)
    smooth_stage(1)

    def body(t, carry):
        colour_stage(t - 2)
        index_stage(t - 1)
        across_stage(t - 1)
        smooth_stage(t)
        return carry

    lax.fori_loop(2, steps, body, 0)
    colour_stage(steps - 2)
    index_stage(steps - 1)
    across_stage(steps - 1)
    colour_stage(steps - 1)


def second_kernel(groups, slab, blocks, haloed, joins, *refs):
    own, refs = refs[:blocks], refs[blocks:]
    halos, refs = (refs[:2], refs[2:]) if haloed else ((), refs)
    (lhs_ref, c_ref), (zin, sm, sems) = refs[:2], refs[-3:]
    image_ref, outs = (refs[2], refs[3:-3]) if joins else (None, refs[2:-3])
    copies = gather_rows(groups, slab, 0, own, halos, zin, None, sems)
    planes = zin.shape[0] - 2 * RAD
    rows = sm.shape[1]
    step = 8

    clear_ends(zin, RAD)
    for copy in copies:
        copy.wait()

    def march(t, carry):
        start = pl.multiple_of(t * step, step)
        stack = plane_smooth(zin, start, step)
        for q in range(0, step, 2):
            out = mxu(lhs_ref[...], jnp.concatenate([stack[q], stack[q + 1]], axis=1))
            sm[q] = out[:, :LANES]
            sm[q + 1] = out[:, LANES:]
        through, red, green, blue = carry
        for i in range(step):
            sigmoid = 0.5 * jnp.tanh(sm[i]) + 0.5
            passed = through * jnp.exp(-(c_ref[3, start + i] * sigmoid))
            weight = through - passed
            red = red + weight * c_ref[0, start + i]
            green = green + weight * c_ref[1, start + i]
            blue = blue + weight * c_ref[2, start + i]
            through = passed
        return through, red, green, blue

    zero = jnp.zeros((rows, LANES), jnp.float32)
    through, red, green, blue = lax.fori_loop(
        0, planes // step, march, (zero + 1.0, zero, zero, zero)
    )
    first = lax.rem(lax.axis_index(GROUP), groups) == 0
    for c, value in enumerate((red, green, blue, through)):
        if joins:
            strips = (
                jnp.concatenate([value[:8], image_ref[c, :8]], axis=0),
                jnp.concatenate([image_ref[c, 8:], value[8:]], axis=0),
            )
            outs[0][c] = jnp.where(first, strips[0], strips[1])
            outs[1][c] = jnp.where(first, strips[1], strips[0])
        else:
            outs[0][c] = value


def vmem_call(kernel, shapes, scratch, in_specs, microseconds, limit):
    return pl.pallas_call(
        kernel,
        in_specs=in_specs,
        out_specs=[pl.BlockSpec(memory_space=pltpu.VMEM)] * len(shapes),
        out_shape=[jax.ShapeDtypeStruct(shape, jnp.float32) for shape in shapes],
        scratch_shapes=scratch,
        compiler_params=pltpu.CompilerParams(vmem_limit_bytes=limit << 20),
        cost_estimate=cost(microseconds),
    )


def exchange(blocks, order):
    blocks = list(blocks)
    got = blocks[:1] + [None] * (len(blocks) - 1)
    for m in order:
        pairs = [(s, s ^ m) for s in range(len(blocks))]
        got[m] = lax.ppermute(blocks[m], GROUP, pairs)
    return got


def row_halo(blocks, groups, count, leads):
    joined = blocks[0].ndim == 4
    total = len(blocks) if joined else len(blocks) // 2
    found = []
    for which in range(2):
        half, member = (0, which) if groups > 1 else (1 - which, 0)
        edge = []
        for i in range(total // groups):
            m = groups * i + member
            if joined:
                low, high = blocks[m][half, :, :RAD], blocks[m][half, :, HALO - RAD :]
                edge.append(jnp.where(leads, low, high) if which else jnp.where(leads, high, low))
            else:
                edge.append(blocks[half * total + m])
        pairs = []
        for strip in range(count):
            for g in range(groups):
                other = strip + (1 if (g == groups - 1) == (which == 0) else -1)
                if 0 <= other < count:
                    pairs.append((strip * groups + g, other * groups + g))
        found.append(lax.ppermute(jnp.stack(edge), ("strips", "pair"), pairs))
    return found


def three_terms(matrix):
    hi, lo = split_np(matrix)
    return np.concatenate([hi, hi, lo], axis=1)


def local(depth, count, groups, fields, colour_palette, opacity_palette, tf_index):
    slab, strip, _ = fields.shape[1:]
    extra = slab // PER
    planes = slab * depth
    rows = strip * groups
    wide = rows + 2 * HALO
    bins = tf_index.shape[0]
    blocks = depth * groups

    bands = jnp.asarray(np.stack(split_np(band(S_TAPS, 2 * LANES, 4 * LANES, LANES).T)))
    smooth_rows = band(S_TAPS, rows + 2 * RAD, wide, HALO - RAD)
    slope_rows = band(D_TAPS, rows, rows + 2 * RAD, RAD)
    inner = slice(HALO, rows - HALO)
    outer = np.r_[0:HALO, rows - HALO : rows]
    forms = []
    for case in range(4):
        inside = np.ones((rows + 2 * RAD, 1))
        if case & 1:
            inside[:RAD] = 0
        if case & 2:
            inside[-RAD:] = 0
        smooth, gradient = smooth_rows[RAD:-RAD], slope_rows @ (inside * smooth_rows)
        forms.append(three_terms(np.concatenate([smooth, gradient], axis=0)))
    edge_form = three_terms(smooth[outer])
    inner_form = three_terms(smooth[inner][:, HALO:-HALO])
    form = jnp.asarray(np.stack(forms))
    across = np.zeros((2 * LANES, LANES))
    across[:LANES] = band(D_TAPS, LANES, LANES, 0).T
    for lane in range(LANES):
        for k in range(-RAD, RAD + 1):
            if lane + k < 0:
                across[LANES + lane + k + RAD, lane] = D_TAPS[k + RAD]
            if lane + k >= LANES:
                across[LANES + RAD + lane + k - LANES, lane] = D_TAPS[k + RAD]
    yw = np.concatenate(split_np(across), axis=1)
    zh, zl = split_np(np.kron(band(S_TAPS, PER, 3 * PER, PER).T, np.eye(2 * RAD)))

    following = jnp.concatenate([tf_index[1:], tf_index[-1:]])
    pair = (tf_index + LANES * following).reshape(bins // LANES, 1, LANES)
    palette = jnp.concatenate([colour_palette, opacity_palette[None]], axis=0)
    palette = jnp.pad(palette, ((0, 0), (0, LANES - palette.shape[1])))[:, None, :]

    anywhere = pl.BlockSpec(memory_space=pl.ANY)
    vmem = pl.BlockSpec(memory_space=pltpu.VMEM)
    f32 = jnp.float32

    def colours(own, halos, lhs):
        shapes = [(4, planes, len(outer), LANES)]
        if rows > len(outer):
            shapes.append((4, planes, rows - len(outer), LANES))
        return vmem_call(
            functools.partial(first_kernel, groups, slab, extra, blocks, count, 1.5 * (2.0 / planes)),
            shapes,
            [
                pltpu.VMEM((planes + 2 * RAD, wide, LANES), f32),
                pltpu.VMEM((planes // PER + 2, wide, LANES), f32),
                pltpu.VMEM((planes + 2 * RAD, rows, LANES), f32),
                pltpu.VMEM((planes, rows, LANES), f32),
                pltpu.VMEM((planes, rows, LANES), f32),
                pltpu.VMEM((planes // PER, rows, LANES), f32),
                pltpu.VMEM((2, 8, rows, LANES), jnp.int32),
                pltpu.VMEM((2, 8, rows, LANES), f32),
                pltpu.SemaphoreType.DMA((4 * (blocks + depth),)),
            ],
            [anywhere] * (2 * blocks + 2) + [vmem] * 6,
            20,
            16,
        )(*own, *halos, lhs, yw, zh, zl, pair, palette)

    def march(own, halos, lhs, coloured, *others):
        mine, out = (wide, len(outer)) if halos else (rows, rows - len(outer))
        return vmem_call(
            functools.partial(second_kernel, groups, slab, blocks, bool(halos), bool(others)),
            [(4, out, LANES)] * (1 + len(others)),
            [
                pltpu.VMEM((planes + 2 * RAD, mine, LANES), f32),
                pltpu.VMEM((8, out, LANES), f32),
                pltpu.SemaphoreType.DMA((2 * blocks,)),
            ],
            [anywhere] * blocks + [vmem] * (len(halos) + 2 + len(others)),
            5,
            10,
        )(*own, *halos, lhs, coloured, *others)

    order = sorted(range(1, blocks), key=lambda m: (bin(m).count("1"), m))
    sent0 = list(source(fields, 0, groups, bands, True, False, 60 << 20))
    leads = sent0.pop()[0] > 0.5
    got0 = exchange(sent0[:blocks], order) + exchange(sent0[blocks:], order)
    sent1 = source(fields, 1, groups, bands, False, True, 58 << 20)
    halo0 = row_halo(got0, groups, count, leads)
    got1 = exchange(sent1, order)
    halo1 = row_halo(got1, groups, count, leads)
    coloured = colours(got0, halo0, form)
    others = ()
    if rows > len(outer):
        others = march(got1, (), inner_form, coloured[1])
    image = march(got1, halo1, edge_form, coloured[0], *others)
    if groups == 1:
        return image[0]
    given = lax.ppermute(image[1], "pair", [(0, 1), (1, 0)])
    return jnp.concatenate(
        [jnp.where(leads, given, image[0]), jnp.where(leads, image[0], given)], axis=2
    )


def solution(mesh):
    depth, tiles = mesh.devices.shape

    def program(fields, colour_palette, opacity_palette, tf_index):
        groups = max(1, fields.shape[3] // (LANES * depth))
        count = tiles // groups
        finer = Mesh(mesh.devices.reshape(depth, count, groups), ("depth", "strips", "pair"))

        def body(*arrays):
            return local(depth, count, groups, *arrays)

        mapped = jax.shard_map(
            body,
            mesh=finer,
            in_specs=(P(None, "depth", ("strips", "pair"), None), P(), P(), P()),
            out_specs=P(None, ("strips", "pair"), "depth"),
            check_vma=False,
        )
        return mapped(fields, colour_palette, opacity_palette, tf_index)

    return program
```

```python
import functools

import jax
import jax.numpy as jnp
import ml_dtypes
import numpy as np
from jax import lax
from jax.experimental import pallas as pl
from jax.experimental.pallas import tpu as pltpu
from jax.sharding import Mesh
from jax.sharding import PartitionSpec as P


RAD = 4
LANES = 128
HALO = 8
GROUP = ("depth", "pair")
PER = LANES // (2 * RAD)

offsets = np.arange(-4.0, 5.0)
bell = np.exp(-(offsets**2) / 8.0)
S_TAPS = bell / np.sqrt(np.sum(bell**2))
slope_raw = offsets * bell
D_TAPS = slope_raw / np.sqrt(np.sum(slope_raw**2))


def split_np(matrix):
    hi = matrix.astype(ml_dtypes.bfloat16)
    lo = (matrix - hi.astype(np.float64)).astype(ml_dtypes.bfloat16)
    return hi, lo


def split(value):
    hi = value.astype(jnp.bfloat16)
    return hi, (value - hi.astype(jnp.float32)).astype(jnp.bfloat16)


def mxu(a, b):
    return jnp.dot(a, b, preferred_element_type=jnp.float32)


def band(taps, rows, cols, shift):
    matrix = np.zeros((rows, cols))
    for row in range(rows):
        for k in range(-RAD, RAD + 1):
            if 0 <= row + k + shift < cols:
                matrix[row, row + k + shift] = taps[k + RAD]
    return matrix


def symmetric(block, n):
    t = [float(x) for x in S_TAPS[RAD:]]
    out = t[0] * block[4 : 4 + n]
    for k in range(1, RAD + 1):
        out = out + t[k] * (block[4 - k : 4 - k + n] + block[4 + k : 4 + k + n])
    return out


def slope(block, n):
    t = [float(x) for x in D_TAPS[RAD:]]
    out = t[1] * (block[5 : 5 + n] - block[3 : 3 + n])
    for k in range(2, RAD + 1):
        out = out + t[k] * (block[4 + k : 4 + k + n] - block[4 - k : 4 - k + n])
    return out


def source_kernel(blocks, groups, which, edges, planes, *refs):
    fields_ref, bands_ref = refs[:2]
    outs, (held, bands, us, ev, in_sems, sems) = refs[2:-6], refs[-6:]
    if edges:
        flag_ref, outs = outs[-1], outs[:-1]
    joined = len(outs) == blocks
    slab, rows, columns = held.shape
    steps = slab // planes
    wide = 2 * LANES

    def fetch(step):
        part = pl.ds(step * planes, planes)
        return pltpu.make_async_copy(fields_ref.at[which, part], held.at[part], in_sems.at[step])

    matrices = pltpu.make_async_copy(bands_ref, bands, in_sems.at[steps])
    fetch(0).start()
    matrices.start()
    for step in range(1, steps):
        fetch(step).start()

    def filtered(step):
        values = held[pl.ds(step * planes, planes)].reshape(planes * rows, columns)
        hi, lo = split(values)
        for j in range(columns // wide):
            left, right = max(0, wide * j - LANES), min(columns, wide * (j + 1) + LANES)
            base = left - (wide * j - LANES)
            bh = bands[0, base : base + right - left]
            bl = bands[1, base : base + right - left]
            u = mxu(hi[:, left:right], bh) + mxu(lo[:, left:right], bh) + mxu(hi[:, left:right], bl)
            for h in range(2):
                us[2 * j + h, pl.ds(step * planes, planes)] = u[
                    :, h * LANES : (h + 1) * LANES
                ].reshape(planes, rows, LANES)

    me = lax.axis_index(GROUP)
    place = lax.rem(me, groups)

    if edges:
        flag_ref[...] = jnp.zeros(flag_ref.shape, jnp.float32) + (place == groups - 1).astype(jnp.float32)

    def copies(at, origin, start, first, count):
        found = []
        for m in range(blocks):
            for h in range(2):
                row = pl.multiple_of(HALO * (h ^ place), HALO)
                target = outs[m].at[h] if joined else outs[h * blocks + m]
                found.append(
                    pltpu.make_async_copy(
                        origin.at[me ^ m, pl.ds(start, count), pl.ds(row, HALO)],
                        target.at[pl.ds(first, count)],
                        sems.at[at, 2 * m + h],
                    )
                )
        return found

    def collected(step):
        lane = lax.broadcasted_iota(jnp.int32, (rows, LANES), 1)
        zero = jnp.zeros((rows, LANES), jnp.float32)
        part = lax.rem(step, PER // planes) * planes
        at = step * planes // PER
        for b in range(blocks):
            acc = ev[b, at]
            for z in range(planes):
                before = us[b - 1, step * planes + z] if b > 0 else zero
                after = us[b + 1, step * planes + z] if b < blocks - 1 else zero
                both = jnp.where(lane >= LANES // 2, before, after)
                moved = pltpu.roll(both, lax.rem(RAD + 2 * RAD * (z + part), LANES), 1)
                acc = jnp.where(lane // (2 * RAD) == z + part, moved, acc)
            ev[b, at] = acc

    def body(step, carry):
        fetch(step).wait()
        filtered(step)
        for copy in copies(step, us, step * planes, step * planes, planes):
            copy.start()
        if edges:
            collected(step)
        return carry

    matrices.wait()
    lax.fori_loop(0, steps, body, 0)
    last = copies(steps, ev, 0, slab, edges) if edges else []
    for copy in last:
        copy.start()
    for at in range(steps):
        for copy in copies(at, us, at * planes, at * planes, planes):
            copy.wait()
    for copy in last:
        copy.wait()


def source(fields, which, groups, bands, edges, joined, vmem):
    _, slab, rows, columns = fields.shape
    blocks = columns // LANES
    extra = slab // PER if edges else 0
    planes = 8
    steps = slab // planes
    block = (slab + extra, HALO, LANES)
    shapes = [(2,) + block] * blocks if joined else [block] * (2 * blocks)
    flag_spec = [pl.BlockSpec(memory_space=pltpu.VMEM)] if edges else []
    flag_shape = [(8, LANES)] if edges else []
    return pl.pallas_call(
        functools.partial(source_kernel, blocks, groups, which, extra, planes),
        in_specs=[pl.BlockSpec(memory_space=pltpu.HBM)] * 2,
        out_specs=[pl.BlockSpec(memory_space=pl.ANY)] * len(shapes) + flag_spec,
        out_shape=[jax.ShapeDtypeStruct(shape, jnp.float32) for shape in shapes + flag_shape],
        scratch_shapes=[
            pltpu.VMEM((slab, rows, columns), jnp.float32),
            pltpu.VMEM(bands.shape, jnp.bfloat16),
            pltpu.VMEM((blocks, slab, rows, LANES), jnp.float32),
            pltpu.VMEM((blocks, max(extra, 1), rows, LANES), jnp.float32),
            pltpu.SemaphoreType.DMA((steps + 1,)),
            pltpu.SemaphoreType.DMA((steps + 1, 2 * blocks)),
        ],
        compiler_params=pltpu.CompilerParams(vmem_limit_bytes=vmem),
        cost_estimate=cost(5),
        name="columns_filter",
    )(fields, bands)


def cost(microseconds):
    return pl.CostEstimate(flops=0, bytes_accessed=int(microseconds * 3e6), transcendentals=0)


def gather_rows(groups, slab, extra, own, halos, zin, ein, sems):
    me = lax.axis_index(GROUP)
    first = HALO if halos else 0
    parts = []
    joined = len(own[0].shape) == 4
    blocks = len(own) if joined else len(own) // 2
    for m in range(blocks):
        d, g = (me ^ m) // groups, lax.rem(me ^ m, groups)
        for h in range(2):
            ref = own[m].at[h] if joined else own[h * blocks + m]
            parts.append((ref, d, first + HALO * (2 * g + (h ^ g))))
    end = zin.shape[1] - HALO
    leads = lax.rem(me, groups) == groups - 1
    narrow = halos and halos[0].shape[2] < HALO
    if halos and not narrow:
        for i in range(halos[0].shape[0]):
            d = (me // groups) ^ i
            parts.append((halos[0].at[i], d, jnp.where(leads, 0, end)))
            parts.append((halos[1].at[i], d, jnp.where(leads, end, 0)))
    copies = []
    for ref, d, row in parts:
        row = pl.multiple_of(row, HALO)
        copies.append(
            pltpu.make_async_copy(
                ref.at[pl.ds(0, slab)],
                zin.at[pl.ds(RAD + d * slab, slab), pl.ds(row, HALO)],
                sems.at[len(copies)],
            )
        )
        if extra:
            copies.append(
                pltpu.make_async_copy(
                    ref.at[pl.ds(slab, extra)],
                    ein.at[pl.ds(1 + d * extra, extra), pl.ds(row, HALO)],
                    sems.at[len(copies)],
                )
            )
    for copy in copies:
        copy.start()
    if narrow:
        for i in range(halos[0].shape[0]):
            part = pl.ds(RAD + ((me // groups) ^ i) * slab, slab)
            one, other = halos[0][i], halos[1][i]
            zin[part, HALO - RAD : HALO, :] = jnp.where(leads, one, other)
            zin[part, end : end + RAD, :] = jnp.where(leads, other, one)
    return copies


def clear_ends(ref, width):
    zero = jnp.zeros((width,) + ref.shape[1:], jnp.float32)
    ref[:width] = zero
    ref[ref.shape[0] - width :] = zero


def plane_smooth(zin, start, count):
    tiles = []
    for row in range(0, zin.shape[1], 8):
        tiles.append(symmetric(zin[pl.ds(start, count + 2 * RAD), row : row + 8, :], count))
    hi, lo = split(jnp.concatenate(tiles, axis=1))
    return jnp.concatenate([hi, lo, hi], axis=1)


def lookup(tables, index):
    return [jnp.take_along_axis(t, index, axis=1, mode="promise_in_bounds") for t in tables]


def first_kernel(groups, slab, extra, blocks, count_strips, factor, *refs):
    own, halos, refs = refs[: 2 * blocks], refs[2 * blocks : 2 * blocks + 2], refs[2 * blocks + 2 :]
    lhs_ref, yw_ref, zh_ref, zl_ref, bins_ref, colour_ref, opacity_ref = refs[:7]
    outs = refs[7:-11]
    zin, ein, sm, gx, gy, es, found_ref, fraction_ref, pair_ref, pal_ref, sems = refs[-11:]
    copies = gather_rows(groups, slab, extra, own, halos, zin, ein, sems)
    planes = zin.shape[0] - 2 * RAD
    rows = sm.shape[1]
    wide = zin.shape[1]
    place = lax.axis_index("strips")
    case = (place == 0).astype(jnp.int32) + 2 * (place == count_strips - 1).astype(jnp.int32)
    lhs_ref = lhs_ref.at[case]
    clear_ends(zin, RAD)
    clear_ends(sm, RAD)
    clear_ends(ein, 1)

    halves = bins_ref.shape[0]
    lane = lax.broadcasted_iota(jnp.int32, (8, LANES), 1)
    held = [jnp.broadcast_to(bins_ref[h : h + 1], (8, LANES)) for h in range(halves)]
    moved = [pltpu.roll(value, LANES - 1, 1) for value in held]
    for h in range(halves):
        following = jnp.where(lane == LANES - 1, moved[min(h + 1, halves - 1)], moved[h])
        pair_ref[h] = held[h] + LANES * following
    pal_ref[...] = jnp.zeros(pal_ref.shape, jnp.float32)
    colours_held = colour_ref.shape[1]
    for c in range(3):
        pal_ref[c, :, :colours_held] = jnp.broadcast_to(colour_ref[c : c + 1], (8, colours_held))
    pal_ref[3, :, :colours_held] = jnp.broadcast_to(opacity_ref[...] * factor, (8, colours_held))
    for copy in copies:
        copy.wait()
    step = 8

    near = [ein[j] for j in range(ein.shape[0])]
    count = len(near) - 2
    stacked = jnp.concatenate(
        [jnp.concatenate(near[k : k + count], axis=0) for k in range(3)], axis=1
    )
    hi, lo = split(stacked)
    ez = mxu(hi, zh_ref[...]) + mxu(lo, zh_ref[...]) + mxu(hi, zl_ref[...])
    hi, lo = split(ez.reshape(count, wide, LANES))
    stack = jnp.concatenate([hi, lo, hi], axis=1)
    for j in range(0, count, 2):
        out = mxu(lhs_ref[:rows], jnp.concatenate([stack[j], stack[j + 1]], axis=1))
        es[j] = out[:, :LANES]
        es[j + 1] = out[:, LANES:]

    def smooth_stage(t):
        start = pl.multiple_of(t * step, step)
        stack = plane_smooth(zin, start, step)
        for q in range(0, step, 2):
            out = mxu(lhs_ref[...], jnp.concatenate([stack[q], stack[q + 1]], axis=1))
            for h in range(2):
                part = out[:, h * LANES : (h + 1) * LANES]
                sm[RAD + start + q + h] = part[:rows]
                gx[start + q + h] = part[rows:]

    def across_stage(t):
        start = pl.multiple_of(t * step, step)
        group = es[start // PER]
        moved = []
        for i in range(step):
            shift = (LANES - 2 * RAD * (lax.rem(start, PER) + i)) % LANES
            moved.append(pltpu.roll(group, shift, 1))
        moved = jnp.concatenate(moved, axis=0)
        own_rows = sm[pl.ds(RAD + start, step)].reshape(step * rows, LANES)
        hi, lo = split(jnp.concatenate([own_rows, moved], axis=1))
        out = mxu(hi, yw_ref[...])
        out = out[:, :LANES] + out[:, LANES:] + mxu(lo, yw_ref[:, :LANES])
        gy[pl.ds(start, step)] = out.reshape(step, rows, LANES)

    bins = halves * LANES
    half = 0.5 * (bins - 1)

    def index_stage(t):
        start = pl.multiple_of(t * step, step)
        pairs = [pair_ref[h] for h in range(halves)]
        for row in range(0, rows, 8):
            level = half * jnp.tanh(0.75 * sm[pl.ds(RAD + start, step), row : row + 8, :]) + half
            index = jnp.minimum(level.astype(jnp.int32), bins - 2)
            fraction_ref[t & 1, :, row : row + 8, :] = level - index.astype(jnp.float32)
            at = index & (LANES - 1)
            found = [lookup(pairs, at[i]) for i in range(step)]
            for i in range(step):
                pair = found[i][0]
                for h in range(1, halves):
                    pair = jnp.where(index[i] >= h * LANES, found[i][h], pair)
                found_ref[t & 1, i, row : row + 8, :] = pair

    def colour_stage(t):
        start = pl.multiple_of(t * step, step)
        colours = [pal_ref[c] for c in range(4)]
        for row in range(0, rows, 8):
            if row == 0 or row == rows - 8:
                o_ref, at = outs[0], min(row, 8)
            else:
                o_ref, at = outs[1], row - 8
            pair = found_ref[t & 1, :, row : row + 8, :]
            fraction = fraction_ref[t & 1, :, row : row + 8, :]
            low, high = pair & (LANES - 1), pair >> 7
            first = [lookup(colours, low[i]) for i in range(step)]
            second = [lookup(colours, high[i]) for i in range(step)]
            grad_z = slope(sm[pl.ds(start, step + 2 * RAD), row : row + 8, :], step)
            grad_x = gx[pl.ds(start, step), row : row + 8, :]
            grad_y = gy[pl.ds(start, step), row : row + 8, :]
            facing = jnp.abs(
                (0.7 * 0.26726) * grad_z + (0.7 * 0.53452) * grad_x + (0.7 * 0.80178) * grad_y
            )
            square = jnp.maximum(grad_z * grad_z + grad_x * grad_x + grad_y * grad_y, 0.1)
            shade = 0.3 + facing * lax.rsqrt(square)
            upper = shade * fraction
            lower = shade - upper
            for i in range(step):
                for c in range(3):
                    o_ref[c, start + i, at : at + 8, :] = first[i][c] * lower[i] + second[i][c] * upper[i]
                o_ref[3, start + i, at : at + 8, :] = first[i][3] + fraction[i] * (
                    second[i][3] - first[i][3]
                )

    steps = planes // step
    smooth_stage(0)
    index_stage(0)
    across_stage(0)
    smooth_stage(1)

    def body(t, carry):
        colour_stage(t - 2)
        index_stage(t - 1)
        across_stage(t - 1)
        smooth_stage(t)
        return carry

    lax.fori_loop(2, steps, body, 0)
    colour_stage(steps - 2)
    index_stage(steps - 1)
    across_stage(steps - 1)
    colour_stage(steps - 1)


def composite(smooth, c_ref, start, carry):
    through, red, green, blue = carry
    for i in range(len(smooth)):
        sigmoid = 0.5 * jnp.tanh(smooth[i]) + 0.5
        passed = through * jnp.exp(-(c_ref[3, start + i] * sigmoid))
        weight = through - passed
        red = red + weight * c_ref[0, start + i]
        green = green + weight * c_ref[1, start + i]
        blue = blue + weight * c_ref[2, start + i]
        through = passed
    return through, red, green, blue


def marched(step_of, planes, rows):
    zero = jnp.zeros((rows, LANES), jnp.float32)
    through, red, green, blue = lax.fori_loop(
        0, planes // 8, step_of, (zero + 1.0, zero, zero, zero)
    )
    return red, green, blue, through


def second_kernel(groups, slab, blocks, haloed, *refs):
    own, refs = refs[:blocks], refs[blocks:]
    halos, refs = (refs[:2], refs[2:]) if haloed else ((), refs)
    (lhs_ref, c_ref), outs, (zin, sm, sems) = refs[:2], refs[2:-3], refs[-3:]
    copies = gather_rows(groups, slab, 0, own, halos, zin, None, sems)
    planes = zin.shape[0] - 2 * RAD
    rows = outs[0].shape[1]
    step = 8
    clear_ends(zin, RAD)
    for copy in copies:
        copy.wait()

    def march(t, carry):
        start = pl.multiple_of(t * step, step)
        stack = plane_smooth(zin, start, step)
        for q in range(0, step, 2):
            out = mxu(lhs_ref[...], jnp.concatenate([stack[q], stack[q + 1]], axis=1))
            for h in range(2):
                part = out[:, h * LANES : (h + 1) * LANES]
                sm[q + h] = part[:rows]
                if len(outs) > 1:
                    outs[1][start + q + h] = part[rows:]
        return composite([sm[i] for i in range(step)], c_ref, start, carry)

    for c, value in enumerate(marched(march, planes, rows)):
        outs[0][c] = value


def edge_kernel(groups, slab, one_ref, other_ref, lhs_ref, c_ref, part_ref, image_ref, *refs):
    kept_ref, sent_ref, zin = refs
    planes = zin.shape[0] - 2 * RAD
    me = lax.axis_index(GROUP)
    leads = lax.rem(me, groups) == groups - 1
    clear_ends(zin, RAD)
    for i in range(one_ref.shape[0]):
        one, other = one_ref[i], other_ref[i]
        zin[pl.ds(RAD + ((me // groups) ^ i) * slab, slab)] = jnp.concatenate(
            [jnp.where(leads, one, other), jnp.where(leads, other, one)], axis=1
        )
    rows = part_ref.shape[1]
    step = 8

    def march(t, carry):
        start = pl.multiple_of(t * step, step)
        sums = symmetric(zin[pl.ds(start, step + 2 * RAD)], step)
        hi, lo = split(sums)
        hi, lo = hi.astype(jnp.float32), lo.astype(jnp.float32)
        stack = jnp.concatenate([hi, lo, hi, jnp.zeros_like(hi)], axis=1).astype(jnp.bfloat16)
        smooth = []
        for q in range(0, step, 2):
            out = mxu(lhs_ref[...], jnp.concatenate([stack[q], stack[q + 1]], axis=1))
            smooth.append(part_ref[start + q] + out[:, :LANES])
            smooth.append(part_ref[start + q + 1] + out[:, LANES:])
        return composite(smooth, c_ref, start, carry)

    first = lax.rem(me, groups) == 0
    for c, value in enumerate(marched(march, planes, rows)):
        strips = (
            jnp.concatenate([value[:8], image_ref[c, :8]], axis=0),
            jnp.concatenate([image_ref[c, 8:], value[8:]], axis=0),
        )
        kept_ref[c] = jnp.where(first, strips[0], strips[1])
        sent_ref[c] = jnp.where(first, strips[1], strips[0])


def vmem_call(kernel, shapes, scratch, in_specs, microseconds, limit):
    return pl.pallas_call(
        kernel,
        in_specs=in_specs,
        out_specs=[pl.BlockSpec(memory_space=pltpu.VMEM)] * len(shapes),
        out_shape=[jax.ShapeDtypeStruct(shape, jnp.float32) for shape in shapes],
        scratch_shapes=scratch,
        compiler_params=pltpu.CompilerParams(vmem_limit_bytes=limit << 20),
        cost_estimate=cost(microseconds),
    )


def exchange(blocks, order):
    blocks = list(blocks)
    got = blocks[:1] + [None] * (len(blocks) - 1)
    for m in order:
        pairs = [(s, s ^ m) for s in range(len(blocks))]
        got[m] = lax.ppermute(blocks[m], GROUP, pairs)
    return got


def row_halo(blocks, groups, count, leads):
    joined = blocks[0].ndim == 4
    total = len(blocks) if joined else len(blocks) // 2
    found = []
    for which in range(2):
        half, member = (0, which) if groups > 1 else (1 - which, 0)
        edge = []
        for i in range(total // groups):
            m = groups * i + member
            if joined:
                low, high = blocks[m][half, :, :RAD], blocks[m][half, :, HALO - RAD :]
                edge.append(jnp.where(leads, low, high) if which else jnp.where(leads, high, low))
            else:
                edge.append(blocks[half * total + m])
        pairs = []
        for strip in range(count):
            for g in range(groups):
                other = strip + (1 if (g == groups - 1) == (which == 0) else -1)
                if 0 <= other < count:
                    pairs.append((strip * groups + g, other * groups + g))
        found.append(lax.ppermute(jnp.stack(edge), ("strips", "pair"), pairs))
    return found


def three_terms(matrix):
    hi, lo = split_np(matrix)
    return np.concatenate([hi, hi, lo], axis=1)


def local(depth, count, groups, fields, colour_palette, opacity_palette, tf_index):
    slab, strip, _ = fields.shape[1:]
    extra = slab // PER
    planes = slab * depth
    rows = strip * groups
    wide = rows + 2 * HALO
    bins = tf_index.shape[0]
    blocks = depth * groups

    bands = jnp.asarray(np.stack(split_np(band(S_TAPS, 2 * LANES, 4 * LANES, LANES).T)))
    smooth_rows = band(S_TAPS, rows + 2 * RAD, wide, HALO - RAD)
    slope_rows = band(D_TAPS, rows, rows + 2 * RAD, RAD)
    inner = slice(HALO, rows - HALO)
    outer = np.r_[0:HALO, rows - HALO : rows]
    forms = []
    for case in range(4):
        inside = np.ones((rows + 2 * RAD, 1))
        if case & 1:
            inside[:RAD] = 0
        if case & 2:
            inside[-RAD:] = 0
        smooth, gradient = smooth_rows[RAD:-RAD], slope_rows @ (inside * smooth_rows)
        forms.append(three_terms(np.concatenate([smooth, gradient], axis=0)))
    edge_form = three_terms(smooth[outer])
    own_form = three_terms(np.concatenate([smooth[inner], smooth[outer]], axis=0)[:, HALO:-HALO])
    near = np.r_[HALO - RAD : HALO, HALO + rows : HALO + rows + RAD]
    near_form = np.pad(three_terms(smooth[outer][:, near]), ((0, 0), (0, 2 * RAD)))
    form = jnp.asarray(np.stack(forms))
    across = np.zeros((2 * LANES, LANES))
    across[:LANES] = band(D_TAPS, LANES, LANES, 0).T
    for lane in range(LANES):
        for k in range(-RAD, RAD + 1):
            if lane + k < 0:
                across[LANES + lane + k + RAD, lane] = D_TAPS[k + RAD]
            if lane + k >= LANES:
                across[LANES + RAD + lane + k - LANES, lane] = D_TAPS[k + RAD]
    yw = np.concatenate(split_np(across), axis=1)
    zh, zl = split_np(np.kron(band(S_TAPS, PER, 3 * PER, PER).T, np.eye(2 * RAD)))

    bin_rows = tf_index.reshape(bins // LANES, LANES)
    opacity_row = opacity_palette.reshape(1, -1)

    anywhere = pl.BlockSpec(memory_space=pl.ANY)
    vmem = pl.BlockSpec(memory_space=pltpu.VMEM)
    f32 = jnp.float32

    def colours(own, halos, lhs):
        shapes = [(4, planes, len(outer), LANES)]
        if rows > len(outer):
            shapes.append((4, planes, rows - len(outer), LANES))
        return vmem_call(
            functools.partial(first_kernel, groups, slab, extra, blocks, count, 1.5 * (2.0 / planes)),
            shapes,
            [
                pltpu.VMEM((planes + 2 * RAD, wide, LANES), f32),
                pltpu.VMEM((planes // PER + 2, wide, LANES), f32),
                pltpu.VMEM((planes + 2 * RAD, rows, LANES), f32),
                pltpu.VMEM((planes, rows, LANES), f32),
                pltpu.VMEM((planes, rows, LANES), f32),
                pltpu.VMEM((planes // PER, rows, LANES), f32),
                pltpu.VMEM((2, 8, rows, LANES), jnp.int32),
                pltpu.VMEM((2, 8, rows, LANES), f32),
                pltpu.VMEM((bins // LANES, 8, LANES), jnp.int32),
                pltpu.VMEM((4, 8, LANES), f32),
                pltpu.SemaphoreType.DMA((4 * (blocks + depth),)),
            ],
            [anywhere] * (2 * blocks + 2) + [vmem] * 7,
            20,
            16,
        )(*own, *halos, lhs, yw, zh, zl, bin_rows, colour_palette, opacity_row)

    def march(own, halos, lhs, coloured):
        mine, out = (wide, len(outer)) if halos else (rows, rows - len(outer))
        return vmem_call(
            functools.partial(second_kernel, groups, slab, blocks, bool(halos)),
            [(4, out, LANES)] + ([] if halos else [(planes, rows - out, LANES)]),
            [
                pltpu.VMEM((planes + 2 * RAD, mine, LANES), f32),
                pltpu.VMEM((8, out, LANES), f32),
                pltpu.SemaphoreType.DMA((2 * blocks,)),
            ],
            [anywhere] * blocks + [vmem] * (len(halos) + 2),
            5,
            10,
        )(*own, *halos, lhs, coloured)

    def edges(halos, coloured, sums, image):
        return vmem_call(
            functools.partial(edge_kernel, groups, slab),
            [(4, strip, LANES)] * 2,
            [pltpu.VMEM((planes + 2 * RAD, 2 * RAD, LANES), f32)],
            [vmem] * 6,
            3,
            10,
        )(*halos, near_form, coloured, sums, image)

    order = sorted(range(1, blocks), key=lambda m: (bin(m).count("1"), m))
    sent0 = list(source(fields, 0, groups, bands, True, False, 60 << 20))
    leads = sent0.pop()[0] > 0.5
    got0 = exchange(sent0[:blocks], order) + exchange(sent0[blocks:], order)
    sent1 = source(fields, 1, groups, bands, False, True, 58 << 20)
    halo0 = row_halo(got0, groups, count, leads)
    got1 = exchange(sent1, order)
    halo1 = row_halo(got1, groups, count, leads)
    coloured = colours(got0, halo0, form)
    if groups == 1:
        return march(got1, halo1, edge_form, coloured[0])[0]
    image, sums = march(got1, (), own_form, coloured[1])
    image = edges(halo1, coloured[0], sums, image)
    given = lax.ppermute(image[1], "pair", [(0, 1), (1, 0)])
    return jnp.concatenate(
        [jnp.where(leads, given, image[0]), jnp.where(leads, image[0], given)], axis=2
    )


def solution(mesh):
    depth, tiles = mesh.devices.shape

    def program(fields, colour_palette, opacity_palette, tf_index):
        groups = max(1, fields.shape[3] // (LANES * depth))
        count = tiles // groups
        finer = Mesh(mesh.devices.reshape(depth, count, groups), ("depth", "strips", "pair"))

        def body(*arrays):
            return local(depth, count, groups, *arrays)

        mapped = jax.shard_map(
            body,
            mesh=finer,
            in_specs=(P(None, "depth", ("strips", "pair"), None), P(), P(), P()),
            out_specs=P(None, ("strips", "pair"), "depth"),
            check_vma=False,
        )
        return mapped(fields, colour_palette, opacity_palette, tf_index)

    return program
```
